512 devices in a mesh: half: 2 (over core), dom: 32 (over z, y_lo), slab: 8 (over y_hi, x).
Axes of the slice: x: 4, y: 8 (y_hi: 2, y_lo: 4; y = y_hi * 4 + y_lo), z: 8, core: 2. Of those that a mesh axis runs over, the one named last changes fastest.
Arguments:
- volume: float32 [2, 8192, 400], P('half', 'slab')
- images: bfloat16 [2, 32768, 400], P('half', 'dom'), may hold values from -18 to 18
- tap_index: int32 [2, 8, 8, 32768], P('half', 'slab', None, 'dom'), may hold values from 0 to 1023, as said below
- tap_weight: float32 [2, 8, 8, 32768], P('half', 'slab', None, 'dom'), may hold values from 0.2 to 1
- classes: int32 [2, 512], P('half', 'dom'), may hold values from 0 to 15
- shifts: int32 [2, 2, 512], P('half', None, 'dom'), may hold values from -8 to 8
- defocus: float32 [16], replicated, may hold values from 0.5 to 3
Outputs:
- updated: float32 [2, 8192, 400], P('half', 'slab')
The draws below stay inside these ranges and needn't reach their ends.
Inputs may be any that keep to these rules, and one draw needn't show every extreme that they name: `tap_index`: the 8 taps of one line and slab read 8 consecutive map lines.
All inputs are finite; a program needn't handle non-finite values.
Results may differ from the reference program's by a relative error of at most 0.0035.
Values may be sent and summed in bfloat16 or wider, within the bound.
No kernel may reach another device: no remote copies, remote signals or barrier semaphores. Data moves between devices by JAX's collectives and lax.ppermute only.
A program may use at most 64 MiB of HBM per device.

```python
import math
import jax
import jax.numpy as jnp
from jax import lax

R = 200
LPI = 64
K = 8
CLASSES = 16
LINES_SLAB = 1024
P_DEV = 16
PARTICLES = 512
ROWS = 32768
LINES = 8192
N_DOM = 32
N_SLAB = 8


def draw_volume(key, part):
    key_shared, key_own, key_mix = jax.random.split(key, 3)
    shared = jax.random.normal(key_shared, (1, LINES, 2 * R), jnp.float32)
    own = jax.random.normal(key_own, (2, LINES, 2 * R), jnp.float32)
    mixing = jax.random.uniform(key_mix, (R,), jnp.float32, 0.0, 0.9)
    columns = jnp.concatenate([mixing, mixing])[None, None, :]
    return jnp.sqrt(columns) * shared + jnp.sqrt(1.0 - columns) * own


def draw_tap_index(key, part):
    base = jax.random.randint(key, (2, N_SLAB, 1, ROWS), 0, LINES_SLAB - K + 1)
    return base + jnp.arange(K, dtype=jnp.int32)[None, None, :, None]


def plant(drawn, key, least, largest):
    longest = drawn.shape.index(max(drawn.shape))
    spots = []
    for shift in (0, 1):
        where = [jax.random.randint(jax.random.fold_in(key, axis), (), 0, length) for axis, length in enumerate(drawn.shape)]
        where[longest] = (where[longest] + shift) % drawn.shape[longest]
        spots.append(tuple(where))
    return drawn.at[spots[0]].set(least).at[spots[1]].set(largest)


def shard_levels(key, extent, cuts, least, largest):
    factor_of = 1.0
    for position, shards_of in cuts:
        draws = jax.random.uniform(jax.random.fold_in(jax.random.fold_in(key, 6), position), (shards_of,), jnp.float32, least / len(cuts), largest / len(cuts))
        factor_of = factor_of * jnp.repeat(jnp.exp(draws), extent[position] // shards_of).reshape((-1,) + (1,) * (len(extent) - 1 - position))
    return factor_of


def normal_values(rng, extent, scale, bound, shards=(), kind=jnp.bfloat16):
    values = jax.random.normal(rng, extent, jnp.float32) * scale
    if len(shards) > 0:
        values = shard_levels(rng, extent, shards, -0.22, 0.18) * values
    return jnp.clip(values, min=-bound, max=bound).astype(kind)


def setup_inputs(seed: int = 0) -> dict:
    streams_of = jax.random.split(jax.random.key(seed), 8)
    volume = draw_volume(jax.random.fold_in(streams_of[7], 71), 0)
    images = normal_values(streams_of[1], (2, ROWS, 2 * R), 3.0, 18.0, ((0, 2), (1, 32)))
    tap_index = draw_tap_index(jax.random.fold_in(streams_of[7], 71), 0)
    tap_weight = jnp.clip(0.2 + 0.8 * jax.random.uniform(streams_of[3], (2, N_SLAB, K, ROWS), jnp.float32) ** shard_levels(streams_of[3], (2, N_SLAB, K, ROWS), ((0, 2), (1, 8), (3, 32)), -0.2, 0.2), 0.2, 1.0)
    classes = plant(jax.random.randint(streams_of[4], (2, PARTICLES), 0, CLASSES), jax.random.fold_in(streams_of[4], 1), 0, CLASSES - 1).astype(jnp.int32)
    shifts = plant(jax.random.randint(streams_of[5], (2, 2, PARTICLES), -8, 9), jax.random.fold_in(streams_of[5], 1), -8, 8).astype(jnp.int32)
    defocus = jnp.clip(jnp.exp(jax.random.uniform(streams_of[6], (CLASSES,), jnp.float32, math.log(0.5), math.log(3.0))), 0.5, 3.0)
    return {"volume": volume, "images": images, "tap_index": tap_index, "tap_weight": tap_weight, "classes": classes, "shifts": shifts, "defocus": defocus}


CTF_GAIN = 30.0
PHASE_ZERO = 0.1
STEP_SCALE = 0.5

def line_terms(classes_half, shifts_half, defocus):
    radius = jnp.arange(R, dtype=jnp.float32)
    focus = defocus[classes_half]
    ctf_part = -jnp.sin(CTF_GAIN * focus[:, None] * (radius[None, :] / R) ** 2 + PHASE_ZERO)
    ctf_rows = jnp.repeat(ctf_part, LPI, axis=0)
    theta = jnp.pi * jnp.arange(LPI, dtype=jnp.float32) / LPI
    theta_rows = jnp.tile(theta, classes_half.shape[0])
    shift_x = jnp.repeat(shifts_half[0].astype(jnp.float32), LPI)
    shift_y = jnp.repeat(shifts_half[1].astype(jnp.float32), LPI)
    along = shift_x * jnp.cos(theta_rows) + shift_y * jnp.sin(theta_rows)
    phase = 2.0 * jnp.pi * radius[None, :] * along[:, None] / (2.0 * R)
    return (ctf_rows, jnp.cos(phase), jnp.sin(phase))

def reference(volume, images, tap_index, tap_weight, classes, shifts, defocus):
    step = STEP_SCALE / math.sqrt(P_DEV * LPI * N_DOM * K / LINES_SLAB)
    grads = []
    cands = []
    for half_num in range(2):
        map_low = volume[half_num].astype(jnp.bfloat16)
        weights = tap_weight[half_num].astype(jnp.bfloat16).astype(jnp.float32)
        proj = jnp.zeros((ROWS, 2 * R), jnp.float32)
        for slab_num in range(N_SLAB):
            partial_value = jnp.zeros((ROWS, 2 * R), jnp.float32)
            for tap_num in range(K):
                lines = map_low[slab_num * LINES_SLAB + tap_index[half_num, slab_num, tap_num]]
                partial_value = partial_value + weights[slab_num, tap_num][:, None] * lines.astype(jnp.float32)
            proj = proj + partial_value
        ctf_rows, cosine, sine_part = line_terms(classes[half_num], shifts[half_num], defocus)
        proj_re, proj_im = (proj[:, :R], proj[:, R:])
        data = images[half_num].astype(jnp.float32)
        res_re = ctf_rows * (cosine * proj_re - sine_part * proj_im) - data[:, :R]
        res_im = ctf_rows * (sine_part * proj_re + cosine * proj_im) - data[:, R:]
        back_re = ctf_rows * (cosine * res_re + sine_part * res_im)
        back_im = ctf_rows * (cosine * res_im - sine_part * res_re)
        back = jnp.concatenate([back_re, back_im], axis=1).astype(jnp.bfloat16).astype(jnp.float32)
        pieces = []
        for slab_num in range(N_SLAB):
            piece = jnp.zeros((LINES_SLAB, 2 * R), jnp.float32)
            for tap_num in range(K):
                piece = piece.at[tap_index[half_num, slab_num, tap_num]].add(weights[slab_num, tap_num][:, None] * back)
            pieces.append(piece)
        grad = jnp.concatenate(pieces, axis=0)
        grads.append(grad)
        cands.append(volume[half_num] - step * grad)
    first, second = cands
    num = lax.optimization_barrier(jnp.sum(first[:, :R] * second[:, :R] + first[:, R:] * second[:, R:], axis=0))
    den_first = lax.optimization_barrier(jnp.sum(first[:, :R] ** 2 + first[:, R:] ** 2, axis=0))
    den_second = lax.optimization_barrier(jnp.sum(second[:, :R] ** 2 + second[:, R:] ** 2, axis=0))
    fsc = num / (jnp.sqrt(den_first * den_second) + 1e-06)
    factor = jnp.tile((1.0 + fsc) / 2.0, 2)
    outs = [volume[half_num] - step * factor[None, :] * grads[half_num] for half_num in range(2)]
    return jnp.stack(outs, axis=0)
```

```python
import math

import jax
import jax.numpy as jnp
from jax import lax
from jax.experimental import pallas as pl
from jax.experimental.pallas import tpu as pltpu
from jax.sharding import PartitionSpec as P

LPI = 64
CTF_GAIN = 30.0
PHASE_ZERO = 0.1
STEP_SCALE = 0.5

R = 200
K = 8
N_SLAB = 8
N_DOM = 32
LINES = 1024
ROWS = 1024
RB = R // N_SLAB
SHARE = LINES // N_DOM
STEP = STEP_SCALE / math.sqrt(ROWS * N_DOM * K / LINES)

F32 = jnp.float32
BF16 = jnp.bfloat16

IM = 32
PACKED = 64
TIGHT = 56


def lane_group(shape):
    return lax.broadcasted_iota(jnp.int32, shape, len(shape) - 1) // SHARE


def pack_kernel(map_ref, index_ref, weight_ref, out_ref, block):
    index = index_ref[...]
    weight = weight_ref[...]
    base = jnp.min(index, axis=0, keepdims=True)
    place = lax.broadcasted_iota(jnp.int32, index.shape, 0)
    ordered = jnp.zeros(weight.shape, F32)
    for tap in range(K):
        ordered += jnp.where(place == index[tap : tap + 1] - base, weight[tap : tap + 1], 0.0)
    block[RB:IM, :] = ordered[: K - 1]
    block[IM + RB : IM + RB + 1, :] = ordered[K - 1 :]
    block[IM + RB + 1 : IM + RB + 2, :] = (base >> 4).astype(F32)
    block[IM + RB + 2 : IM + RB + 3, :] = (base & 15).astype(F32)
    block[IM + RB + 3 :, :] = jnp.zeros((PACKED - IM - RB - 3, LINES), F32)
    for part in range(N_SLAB):
        block[:RB, :] = map_ref[RB * part : RB * (part + 1), :]
        block[IM : IM + RB, :] = map_ref[R + RB * part : R + RB * (part + 1), :]
        out_ref[part] = block[...].astype(BF16)


def regroup(tiles, y, group):
    out = None
    for slot, tile in enumerate(tiles):
        moved = pltpu.roll(tile, (SHARE * (slot - y)) % 128, 1)
        out = moved if out is None else jnp.where(group == slot, moved, out)
    return out


def image_kernel(place_ref, packed_ref, data_ref, ctf_ref, cos_ref, sin_ref, out_ref, own_ref, taps, proj, back, grad):
    proj[...] = jnp.zeros(proj.shape, F32)

    @pl.loop(0, N_SLAB)
    def _(slab):
        rows = packed_ref[slab].astype(F32)
        low = rows[IM + RB + 2 : IM + RB + 3]
        line = lax.broadcasted_iota(jnp.int32, (16, ROWS), 0).astype(F32)
        first = jnp.zeros((16, ROWS), F32)
        second = jnp.zeros((16, ROWS), F32)
        for tap in range(K):
            row = RB + tap if tap < K - 1 else IM + RB
            weight = rows[row : row + 1]
            first += jnp.where(line == low + tap, weight, 0.0)
            second += jnp.where(line + 16.0 == low + tap, weight, 0.0)
        first = first.astype(BF16)
        second = second.astype(BF16)
        high = jnp.broadcast_to(rows[IM + RB + 1 : IM + RB + 2], (16, ROWS)).astype(BF16)
        none = jnp.zeros((16, ROWS), BF16)
        before = None
        for chunk in range(LINES // 16):
            here = high == jnp.asarray(chunk, BF16)
            value = jnp.where(here, first, none)
            if before is not None:
                value = jnp.where(before, second, value)
            taps[slab, 16 * chunk : 16 * (chunk + 1), :] = value
            before = here
        proj[...] += jnp.dot(packed_ref[slab], taps[slab], preferred_element_type=F32)

    ctf = ctf_ref[...]
    cosine = cos_ref[...]
    sine = sin_ref[...]
    proj_re = proj[:IM]
    proj_im = proj[IM:]
    res_re = ctf * (cosine * proj_re - sine * proj_im) - data_ref[0].astype(F32)
    res_im = ctf * (sine * proj_re + cosine * proj_im) - data_ref[1].astype(F32)
    back_re = ctf * (cosine * res_re + sine * res_im)
    back_im = ctf * (cosine * res_im - sine * res_re)
    back[2 * RB :, :] = jnp.zeros((TIGHT - 2 * RB, ROWS), F32)
    back[:RB, :] = back_re[:RB]
    back[RB : 2 * RB, :] = back_im[:RB]
    back_low = back[...].astype(BF16)

    @pl.loop(0, N_SLAB)
    def _(slab):
        grad[slab] = lax.dot_general(back_low, taps[slab], (((1,), (1,)), ((), ())), preferred_element_type=F32)

    group = lane_group((TIGHT, 128))
    for z in range(8):
        for half in range(2):
            tiles = [grad[4 * half + slot, :, 128 * z : 128 * (z + 1)] for slot in range(4)]
            for y in range(4):
                out_ref[4 * z + y, half] = regroup(tiles, y, group).astype(BF16)

    z = pl.multiple_of(place_ref[0] * 128, 128)
    y = place_ref[1]
    group = lane_group((PACKED, 128))
    for half in range(2):
        out = None
        for slot in range(4):
            tile = packed_ref[4 * half + slot, :, pl.ds(z, 128)].astype(F32)
            moved = pltpu.roll(tile, (SHARE * (slot - y)) & 127, 1)
            out = moved if out is None else jnp.where(group == slot, moved, out)
        own_ref[half] = out


def reduce_kernel(parts_ref, own_ref, grad_ref, cand_ref, total):
    total[...] = jnp.sum(parts_ref[...].astype(F32), axis=0)
    grad_ref[...] = jnp.zeros(grad_ref.shape, F32)
    grad_ref[:, :RB, :] = total[:, :RB, :]
    grad_ref[:, IM : IM + RB, :] = total[:, RB : 2 * RB, :]
    row = lax.broadcasted_iota(jnp.int32, cand_ref.shape, 1) % IM
    cand_ref[...] = jnp.where(row < RB, own_ref[...] - STEP * grad_ref[...], 0.0)


def shell_kernel(grad_ref, cand_ref, other_ref, out_ref, block):
    mine = cand_ref[...]
    other = other_ref[...]

    def shell(value):
        value = value[0] + value[1]
        return value[:IM] + value[IM:]

    sums = jnp.concatenate([shell(mine * other), shell(mine * mine), shell(other * other), jnp.zeros((IM, 128), F32)], axis=0)
    sums = jnp.sum(sums.T, axis=0, keepdims=True)
    group = lane_group((1, 128))
    block[...] = grad_ref[...]
    for item in range(3):
        row = None
        for slot in range(4):
            moved = pltpu.roll(sums, (IM * (slot - item)) % 128, 1)
            row = moved if row is None else jnp.where(group == slot, moved, row)
        high = row.astype(BF16).astype(F32)
        for half in range(2):
            block[half, RB + 2 * item : RB + 2 * item + 1, :] = high
            block[half, RB + 2 * item + 1 : RB + 2 * item + 2, :] = row - high
    group = lane_group((16, 128))
    for half in range(2):
        tiles = [block[half, 16 * fold : 16 * (fold + 1), :] for fold in range(4)]
        for slot in range(4):
            out_ref[4 * half + slot] = regroup(tiles, slot, group).astype(BF16)


def update_kernel(map_ref, parts_ref, out_ref, scale):
    sums = jnp.zeros((N_SLAB, 16, 128), F32)
    for index in range(N_DOM):
        sums += parts_ref[index].astype(F32)
    first = RB - 16
    num = sums[:, first, :] + sums[:, first + 1, :]
    den_mine = sums[:, first + 2, :] + sums[:, first + 3, :]
    den_other = sums[:, first + 4, :] + sums[:, first + 5, :]
    fsc = num / (jnp.sqrt(den_mine * den_other) + 1e-06)
    factor = STEP * (1.0 + fsc) / 2.0
    factor = jnp.where(lane_group((N_SLAB, 128)) == 1, factor, 0.0)
    factor = jnp.concatenate([factor, jnp.zeros((128 - N_SLAB, 128), F32)], axis=0).T
    scale[...] = factor[SHARE : 2 * SHARE, :]
    group = lane_group((16, 128))

    @pl.loop(0, 8)
    def _(z):
        lanes = pl.ds(pl.multiple_of(z * 128, 128), 128)
        for part in range(N_SLAB):
            tiles = [parts_ref[4 * z + y, part].astype(F32) for y in range(4)]
            for fold in range(4):
                count = 16 if fold % 2 == 0 else RB - 16
                start = 16 * (fold % 2)
                at = R * (fold // 2) + RB * part + start
                value = regroup(tiles, fold, group)
                weight = scale[start : start + 16, part : part + 1]
                out_ref[at : at + count, lanes] = map_ref[at : at + count, lanes] - (weight * value)[:count]


def vmem():
    return pl.BlockSpec(memory_space=pltpu.VMEM)


def exchange(value, axis):
    return lax.all_to_all(value, axis, 0, 0, tiled=True)


def line_terms(classes_local, shifts_local, defocus, radius):
    class_ids = jnp.arange(defocus.shape[0], dtype=jnp.int32)
    focus = jnp.sum(jnp.where(classes_local[:, None] == class_ids[None, :], defocus[None, :], 0.0), axis=1)
    ctf = -jnp.sin(CTF_GAIN * focus[None, :] * (radius[:, None] / R) ** 2 + PHASE_ZERO)
    ctf_rows = jnp.repeat(ctf, LPI, axis=1)
    theta = jnp.pi * jnp.arange(LPI, dtype=F32) / LPI
    theta_rows = jnp.tile(theta, classes_local.shape[0])
    shift_x = jnp.repeat(shifts_local[0].astype(F32), LPI)
    shift_y = jnp.repeat(shifts_local[1].astype(F32), LPI)
    along = shift_x * jnp.cos(theta_rows) + shift_y * jnp.sin(theta_rows)
    phase = 2.0 * jnp.pi * radius[:, None] * along[None, :] / (2.0 * R)
    return (ctf_rows, jnp.cos(phase), jnp.sin(phase))


def body(volume, images, tap_index, tap_weight, classes, shifts, defocus):
    map_t = volume[0].T
    data_t = images[0].T
    slab = lax.axis_index("slab")
    dom = lax.axis_index("dom")

    packed = pl.pallas_call(
        pack_kernel,
        out_shape=jax.ShapeDtypeStruct((N_SLAB, PACKED, LINES), BF16),
        in_specs=[vmem()] * 3,
        out_specs=vmem(),
        scratch_shapes=[pltpu.VMEM((PACKED, LINES), F32)],
        name="pack",
    )(map_t, tap_index[0, 0], tap_weight[0, 0])
    packed = exchange(packed, "slab")

    pad = ((0, IM - RB), (0, 0))
    radius = (RB * slab + jnp.arange(RB)).astype(F32)
    ctf, cosine, sine = line_terms(classes[0], shifts[0], defocus, radius)
    ctf, cosine, sine = (jnp.pad(ctf, pad), jnp.pad(cosine, pad), jnp.pad(sine, pad))
    data = lax.dynamic_slice(data_t.reshape(2, R, ROWS), (0, RB * slab, 0), (2, RB, ROWS))
    data = jnp.pad(data, ((0, 0),) + pad)
    place = jnp.stack([dom // 4, dom % 4]).astype(jnp.int32)

    parts, own = pl.pallas_call(
        image_kernel,
        out_shape=(
            jax.ShapeDtypeStruct((N_DOM, 2, TIGHT, 128), BF16),
            jax.ShapeDtypeStruct((2, PACKED, 128), F32),
        ),
        in_specs=[pl.BlockSpec(memory_space=pltpu.SMEM)] + [vmem()] * 5,
        out_specs=(vmem(), vmem()),
        scratch_shapes=[
            pltpu.VMEM((N_SLAB, LINES, ROWS), BF16),
            pltpu.VMEM((PACKED, ROWS), F32),
            pltpu.VMEM((TIGHT, ROWS), F32),
            pltpu.VMEM((N_SLAB, TIGHT, LINES), F32),
        ],
        compiler_params=pltpu.CompilerParams(vmem_limit_bytes=48 << 20),
        name="image",
    )(place, packed, data, ctf, cosine, sine)
    parts = exchange(parts, "dom")

    block = jax.ShapeDtypeStruct((2, PACKED, 128), F32)
    grad, cand = pl.pallas_call(
        reduce_kernel,
        out_shape=(block, block),
        in_specs=[vmem()] * 2,
        out_specs=(vmem(), vmem()),
        scratch_shapes=[pltpu.VMEM((2, TIGHT, 128), F32)],
        name="reduce",
    )(parts, own)
    other = lax.ppermute(cand, "half", [(0, 1), (1, 0)])
    share = pl.pallas_call(
        shell_kernel,
        out_shape=jax.ShapeDtypeStruct((N_SLAB, 16, 128), BF16),
        in_specs=[vmem()] * 3,
        out_specs=vmem(),
        scratch_shapes=[pltpu.VMEM((2, PACKED, 128), F32)],
        name="shell",
    )(grad, cand, other)
    share = exchange(share, "slab")
    every = exchange(jnp.broadcast_to(share[None], (N_DOM,) + share.shape), "dom")
    result = pl.pallas_call(
        update_kernel,
        out_shape=jax.ShapeDtypeStruct((2 * R, LINES), F32),
        in_specs=[vmem()] * 2,
        out_specs=vmem(),
        scratch_shapes=[pltpu.VMEM((SHARE, 128), F32)],
        name="update",
    )(map_t, every)
    return result.T[None]


def solution(mesh):
    placed = (
        P("half", "slab", None),
        P("half", "dom", None),
        P("half", "slab", None, "dom"),
        P("half", "slab", None, "dom"),
        P("half", "dom"),
        P("half", None, "dom"),
        P(),
    )
    return jax.shard_map(
        body, mesh=mesh, in_specs=placed, out_specs=P("half", "slab", None), check_vma=False
    )
```

```python
import math

import jax
import jax.numpy as jnp
from jax import lax
from jax.experimental import pallas as pl
from jax.experimental.pallas import tpu as pltpu
from jax.sharding import PartitionSpec as P

LPI = 64
CTF_GAIN = 30.0
PHASE_ZERO = 0.1
STEP_SCALE = 0.5

R = 200
K = 8
N_SLAB = 8
N_DOM = 32
LINES = 1024
ROWS = 1024
RB = R // N_SLAB
SHARE = LINES // N_DOM
STEP = STEP_SCALE / math.sqrt(ROWS * N_DOM * K / LINES)

F32 = jnp.float32
BF16 = jnp.bfloat16

IM = 32
PACKED = 64
TIGHT = 56


def lane_group(shape):
    return lax.broadcasted_iota(jnp.int32, shape, len(shape) - 1) // SHARE


def pack_kernel(map_ref, index_ref, weight_ref, out_ref, block):
    index = index_ref[...]
    weight = weight_ref[...]
    base = jnp.min(index, axis=0, keepdims=True)
    place = lax.broadcasted_iota(jnp.int32, index.shape, 0)
    ordered = jnp.zeros(weight.shape, F32)
    for tap in range(K):
        ordered += jnp.where(place == index[tap : tap + 1] - base, weight[tap : tap + 1], 0.0)
    block[RB:IM, :] = ordered[: K - 1]
    block[IM + RB : IM + RB + 1, :] = ordered[K - 1 :]
    block[IM + RB + 1 : IM + RB + 2, :] = (base >> 4).astype(F32)
    block[IM + RB + 2 : IM + RB + 3, :] = (base & 15).astype(F32)
    block[IM + RB + 3 :, :] = jnp.zeros((PACKED - IM - RB - 3, LINES), F32)
    for part in range(N_SLAB):
        block[:RB, :] = map_ref[RB * part : RB * (part + 1), :]
        block[IM : IM + RB, :] = map_ref[R + RB * part : R + RB * (part + 1), :]
        out_ref[part] = block[...].astype(BF16)


def regroup(tiles, y, group):
    out = None
    for slot, tile in enumerate(tiles):
        moved = pltpu.roll(tile, (SHARE * (slot - y)) % 128, 1)
        out = moved if out is None else jnp.where(group == slot, moved, out)
    return out


def image_kernel(place_ref, packed_ref, data_ref, ctf_ref, cos_ref, sin_ref, out_ref, own_ref, taps, proj, back, grad):
    proj[...] = jnp.zeros(proj.shape, F32)

    @pl.loop(0, N_SLAB)
    def _(slab):
        rows = packed_ref[slab].astype(F32)
        low = rows[IM + RB + 2 : IM + RB + 3]
        line = lax.broadcasted_iota(jnp.int32, (16, ROWS), 0).astype(F32)
        first = jnp.zeros((16, ROWS), F32)
        second = jnp.zeros((16, ROWS), F32)
        for tap in range(K):
            row = RB + tap if tap < K - 1 else IM + RB
            weight = rows[row : row + 1]
            first += jnp.where(line == low + tap, weight, 0.0)
            second += jnp.where(line + 16.0 == low + tap, weight, 0.0)
        first = first.astype(BF16)
        second = second.astype(BF16)
        high = jnp.broadcast_to(rows[IM + RB + 1 : IM + RB + 2], (16, ROWS)).astype(BF16)
        none = jnp.zeros((16, ROWS), BF16)
        before = None
        for chunk in range(LINES // 16):
            here = high == jnp.asarray(chunk, BF16)
            value = jnp.where(here, first, none)
            if before is not None:
                value = jnp.where(before, second, value)
            taps[slab, 16 * chunk : 16 * (chunk + 1), :] = value
            before = here
        proj[...] += jnp.dot(packed_ref[slab], taps[slab], preferred_element_type=F32)

    ctf = ctf_ref[...]
    cosine = cos_ref[...]
    sine = sin_ref[...]
    proj_re = proj[:IM]
    proj_im = proj[IM:]
    res_re = ctf * (cosine * proj_re - sine * proj_im) - data_ref[0].astype(F32)
    res_im = ctf * (sine * proj_re + cosine * proj_im) - data_ref[1].astype(F32)
    back_re = ctf * (cosine * res_re + sine * res_im)
    back_im = ctf * (cosine * res_im - sine * res_re)
    back[2 * RB :, :] = jnp.zeros((TIGHT - 2 * RB, ROWS), F32)
    back[:RB, :] = back_re[:RB]
    back[RB : 2 * RB, :] = back_im[:RB]
    back_low = back[...].astype(BF16)

    @pl.loop(0, N_SLAB)
    def _(slab):
        grad[slab] = lax.dot_general(back_low, taps[slab], (((1,), (1,)), ((), ())), preferred_element_type=F32)

    group = lane_group((TIGHT, 128))
    for z in range(8):
        for half in range(2):
            tiles = [grad[4 * half + slot, :, 128 * z : 128 * (z + 1)] for slot in range(4)]
            for y in range(4):
                out_ref[4 * z + y, half] = regroup(tiles, y, group).astype(BF16)

    z = pl.multiple_of(place_ref[0] * 128, 128)
    y = place_ref[1]
    group = lane_group((PACKED, 128))
    for half in range(2):
        out = None
        for slot in range(4):
            tile = packed_ref[4 * half + slot, :, pl.ds(z, 128)].astype(F32)
            moved = pltpu.roll(tile, (SHARE * (slot - y)) & 127, 1)
            out = moved if out is None else jnp.where(group == slot, moved, out)
        own_ref[half] = out


def reduce_kernel(parts_ref, own_ref, grad_ref, cand_ref, total):
    total[...] = jnp.sum(parts_ref[...].astype(F32), axis=0)
    grad_ref[...] = jnp.zeros(grad_ref.shape, F32)
    grad_ref[:, :RB, :] = total[:, :RB, :]
    grad_ref[:, IM : IM + RB, :] = total[:, RB : 2 * RB, :]
    row = lax.broadcasted_iota(jnp.int32, cand_ref.shape, 1) % IM
    cand_ref[...] = jnp.where(row < RB, own_ref[...] - STEP * grad_ref[...], 0.0)


def shell_kernel(grad_ref, cand_ref, other_ref, out_ref, block):
    mine = cand_ref[...]
    other = other_ref[...]

    def shell(value):
        value = value[0] + value[1]
        return value[:IM] + value[IM:]

    sums = jnp.concatenate([shell(mine * other), shell(mine * mine), shell(other * other), jnp.zeros((IM, 128), F32)], axis=0)
    sums = jnp.sum(sums.T, axis=0, keepdims=True)
    group = lane_group((1, 128))
    block[...] = grad_ref[...]
    for item in range(3):
        row = None
        for slot in range(4):
            moved = pltpu.roll(sums, (IM * (slot - item)) % 128, 1)
            row = moved if row is None else jnp.where(group == slot, moved, row)
        high = row.astype(BF16).astype(F32)
        for half in range(2):
            block[half, RB + 2 * item : RB + 2 * item + 1, :] = high
            block[half, RB + 2 * item + 1 : RB + 2 * item + 2, :] = row - high
    group = lane_group((16, 128))
    for half in range(2):
        tiles = [block[half, 16 * fold : 16 * (fold + 1), :] for fold in range(4)]
        for slot in range(4):
            out_ref[4 * half + slot] = regroup(tiles, slot, group).astype(BF16)


def update_kernel(map_ref, parts_ref, out_ref, scale):
    sums = jnp.zeros((N_SLAB, 16, 128), F32)
    for index in range(N_DOM):
        sums += parts_ref[index].astype(F32)
    first = RB - 16
    num = sums[:, first, :] + sums[:, first + 1, :]
    den_mine = sums[:, first + 2, :] + sums[:, first + 3, :]
    den_other = sums[:, first + 4, :] + sums[:, first + 5, :]
    fsc = num / (jnp.sqrt(den_mine * den_other) + 1e-06)
    factor = STEP * (1.0 + fsc) / 2.0
    factor = jnp.where(lane_group((N_SLAB, 128)) == 1, factor, 0.0)
    factor = jnp.concatenate([factor, jnp.zeros((128 - N_SLAB, 128), F32)], axis=0).T
    scale[...] = factor[SHARE : 2 * SHARE, :]
    group = lane_group((16, 128))

    @pl.loop(0, 8)
    def _(z):
        lanes = pl.ds(pl.multiple_of(z * 128, 128), 128)
        for part in range(N_SLAB):
            tiles = [parts_ref[4 * z + y, part].astype(F32) for y in range(4)]
            for fold in range(4):
                count = 16 if fold % 2 == 0 else RB - 16
                start = 16 * (fold % 2)
                at = R * (fold // 2) + RB * part + start
                value = regroup(tiles, fold, group)
                weight = scale[start : start + 16, part : part + 1]
                out_ref[at : at + count, lanes] = map_ref[at : at + count, lanes] - (weight * value)[:count]


def vmem():
    return pl.BlockSpec(memory_space=pltpu.VMEM)


def limit(mib):
    return pltpu.CompilerParams(vmem_limit_bytes=mib << 20)


def exchange(value, axis):
    flat = value.reshape(value.shape[0], -1, value.shape[-1])
    return lax.all_to_all(flat, axis, 0, 0, tiled=True).reshape(value.shape)


def line_terms(classes_local, shifts_local, defocus, radius):
    class_ids = jnp.arange(defocus.shape[0], dtype=jnp.int32)
    focus = jnp.sum(jnp.where(classes_local[:, None] == class_ids[None, :], defocus[None, :], 0.0), axis=1)
    ctf = -jnp.sin(CTF_GAIN * focus[None, :] * (radius[:, None] / R) ** 2 + PHASE_ZERO)
    ctf_rows = jnp.repeat(ctf, LPI, axis=1)
    theta = jnp.pi * jnp.arange(LPI, dtype=F32) / LPI
    theta_rows = jnp.tile(theta, classes_local.shape[0])
    shift_x = jnp.repeat(shifts_local[0].astype(F32), LPI)
    shift_y = jnp.repeat(shifts_local[1].astype(F32), LPI)
    along = shift_x * jnp.cos(theta_rows) + shift_y * jnp.sin(theta_rows)
    phase = 2.0 * jnp.pi * radius[:, None] * along[None, :] / (2.0 * R)
    return (ctf_rows, jnp.cos(phase), jnp.sin(phase))


def body(volume, images, tap_index, tap_weight, classes, shifts, defocus):
    map_t = volume[0].T
    data_t = images[0].T
    slab = lax.axis_index("slab")
    dom = lax.axis_index("dom")

    packed = pl.pallas_call(
        pack_kernel,
        out_shape=jax.ShapeDtypeStruct((N_SLAB, PACKED, LINES), BF16),
        in_specs=[vmem()] * 3,
        out_specs=vmem(),
        scratch_shapes=[pltpu.VMEM((PACKED, LINES), F32)],
        compiler_params=limit(6),
        name="pack",
    )(map_t, tap_index[0, 0], tap_weight[0, 0])
    packed = exchange(packed, "slab")

    pad = ((0, IM - RB), (0, 0))
    radius = (RB * slab + jnp.arange(RB)).astype(F32)
    ctf, cosine, sine = line_terms(classes[0], shifts[0], defocus, radius)
    ctf, cosine, sine = (jnp.pad(ctf, pad), jnp.pad(cosine, pad), jnp.pad(sine, pad))
    data = lax.dynamic_slice(data_t.reshape(2, R, ROWS), (0, RB * slab, 0), (2, RB, ROWS))
    data = jnp.pad(data, ((0, 0),) + pad)
    place = jnp.stack([dom // 4, dom % 4]).astype(jnp.int32)

    parts, own = pl.pallas_call(
        image_kernel,
        out_shape=(
            jax.ShapeDtypeStruct((N_DOM, 2, TIGHT, 128), BF16),
            jax.ShapeDtypeStruct((2, PACKED, 128), F32),
        ),
        in_specs=[pl.BlockSpec(memory_space=pltpu.SMEM)] + [vmem()] * 5,
        out_specs=(vmem(), vmem()),
        scratch_shapes=[
            pltpu.VMEM((N_SLAB, LINES, ROWS), BF16),
            pltpu.VMEM((PACKED, ROWS), F32),
            pltpu.VMEM((TIGHT, ROWS), F32),
            pltpu.VMEM((N_SLAB, TIGHT, LINES), F32),
        ],
        compiler_params=limit(32),
        name="image",
    )(place, packed, data, ctf, cosine, sine)
    parts = exchange(parts, "dom")

    block = jax.ShapeDtypeStruct((2, PACKED, 128), F32)
    grad, cand = pl.pallas_call(
        reduce_kernel,
        out_shape=(block, block),
        in_specs=[vmem()] * 2,
        out_specs=(vmem(), vmem()),
        scratch_shapes=[pltpu.VMEM((2, TIGHT, 128), F32)],
        compiler_params=limit(4),
        name="reduce",
    )(parts, own)
    other = lax.ppermute(cand, "half", [(0, 1), (1, 0)])
    share = pl.pallas_call(
        shell_kernel,
        out_shape=jax.ShapeDtypeStruct((N_SLAB, 16, 128), BF16),
        in_specs=[vmem()] * 3,
        out_specs=vmem(),
        scratch_shapes=[pltpu.VMEM((2, PACKED, 128), F32)],
        compiler_params=limit(2),
        name="shell",
    )(grad, cand, other)
    share = exchange(share, "slab")
    every = exchange(jnp.broadcast_to(share[None], (N_DOM,) + share.shape), "dom")
    result = pl.pallas_call(
        update_kernel,
        out_shape=jax.ShapeDtypeStruct((2 * R, LINES), F32),
        in_specs=[vmem()] * 2,
        out_specs=vmem(),
        scratch_shapes=[pltpu.VMEM((SHARE, 128), F32)],
        compiler_params=limit(8),
        name="update",
    )(map_t, every)
    return result.T[None]


def solution(mesh):
    placed = (
        P("half", "slab", None),
        P("half", "dom", None),
        P("half", "slab", None, "dom"),
        P("half", "slab", None, "dom"),
        P("half", "dom"),
        P("half", None, "dom"),
        P(),
    )
    return jax.shard_map(
        body, mesh=mesh, in_specs=placed, out_specs=P("half", "slab", None), check_vma=False
    )
```

```python
import math

import jax
import jax.numpy as jnp
from jax import lax
from jax.experimental import pallas as pl
from jax.experimental.pallas import tpu as pltpu
from jax.sharding import PartitionSpec as P

LPI = 64
CTF_GAIN = 30.0
PHASE_ZERO = 0.1
STEP_SCALE = 0.5

R = 200
K = 8
N_SLAB = 8
N_DOM = 32
LINES = 1024
ROWS = 1024
RB = R // N_SLAB
SHARE = LINES // N_DOM
STEP = STEP_SCALE / math.sqrt(ROWS * N_DOM * K / LINES)

F32 = jnp.float32
BF16 = jnp.bfloat16

IM = 32
PACKED = 64
TIGHT = 56


def lane_group(shape):
    return lax.broadcasted_iota(jnp.int32, shape, len(shape) - 1) // SHARE


def pack_kernel(map_ref, index_ref, weight_ref, out_ref, block):
    index = index_ref[...]
    weight = weight_ref[...]
    base = jnp.min(index, axis=0, keepdims=True)
    place = lax.broadcasted_iota(jnp.int32, index.shape, 0)
    ordered = jnp.zeros(weight.shape, F32)
    for tap in range(K):
        ordered += jnp.where(place == index[tap : tap + 1] - base, weight[tap : tap + 1], 0.0)
    block[RB:IM, :] = ordered[: K - 1]
    block[IM + RB : IM + RB + 1, :] = ordered[K - 1 :]
    block[IM + RB + 1 : IM + RB + 2, :] = (base >> 4).astype(F32)
    block[IM + RB + 2 : IM + RB + 3, :] = (base & 15).astype(F32)
    block[IM + RB + 3 :, :] = jnp.zeros((PACKED - IM - RB - 3, LINES), F32)
    for part in range(N_SLAB):
        block[:RB, :] = map_ref[RB * part : RB * (part + 1), :]
        block[IM : IM + RB, :] = map_ref[R + RB * part : R + RB * (part + 1), :]
        out_ref[part] = block[...].astype(BF16)


def regroup(tiles, y, group):
    out = None
    for slot, tile in enumerate(tiles):
        moved = pltpu.roll(tile, (SHARE * (slot - y)) % 128, 1)
        out = moved if out is None else jnp.where(group == slot, moved, out)
    return out


def image_kernel(place_ref, packed_ref, data_ref, ctf_ref, cos_ref, sin_ref, out_ref, own_ref, taps, proj, back, grad):
    proj[...] = jnp.zeros(proj.shape, F32)

    @pl.loop(0, N_SLAB)
    def _(slab):
        rows = packed_ref[slab].astype(F32)
        low = rows[IM + RB + 2 : IM + RB + 3]
        line = lax.broadcasted_iota(jnp.int32, (16, ROWS), 0).astype(F32)
        first = jnp.zeros((16, ROWS), F32)
        second = jnp.zeros((16, ROWS), F32)
        for tap in range(K):
            row = RB + tap if tap < K - 1 else IM + RB
            weight = rows[row : row + 1]
            first += jnp.where(line == low + tap, weight, 0.0)
            second += jnp.where(line + 16.0 == low + tap, weight, 0.0)
        first = first.astype(BF16)
        second = second.astype(BF16)
        high = jnp.broadcast_to(rows[IM + RB + 1 : IM + RB + 2], (16, ROWS)).astype(BF16)
        none = jnp.zeros((16, ROWS), BF16)
        before = None
        for chunk in range(LINES // 16):
            here = high == jnp.asarray(chunk, BF16)
            value = jnp.where(here, first, none)
            if before is not None:
                value = jnp.where(before, second, value)
            taps[slab, 16 * chunk : 16 * (chunk + 1), :] = value
            before = here
        proj[...] += jnp.dot(packed_ref[slab], taps[slab], preferred_element_type=F32)

    ctf = ctf_ref[...]
    cosine = cos_ref[...]
    sine = sin_ref[...]
    proj_re = proj[:IM]
    proj_im = proj[IM:]
    res_re = ctf * (cosine * proj_re - sine * proj_im) - data_ref[0].astype(F32)
    res_im = ctf * (sine * proj_re + cosine * proj_im) - data_ref[1].astype(F32)
    back_re = ctf * (cosine * res_re + sine * res_im)
    back_im = ctf * (cosine * res_im - sine * res_re)
    back[2 * RB :, :] = jnp.zeros((TIGHT - 2 * RB, ROWS), F32)
    back[:RB, :] = back_re[:RB]
    back[RB : 2 * RB, :] = back_im[:RB]
    back_low = back[...].astype(BF16)

    @pl.loop(0, N_SLAB)
    def _(slab):
        grad[slab] = lax.dot_general(back_low, taps[slab], (((1,), (1,)), ((), ())), preferred_element_type=F32)

    group = lane_group((TIGHT, 128))
    for z in range(8):
        for half in range(2):
            tiles = [grad[4 * half + slot, :, 128 * z : 128 * (z + 1)] for slot in range(4)]
            for y in range(4):
                out_ref[4 * z + y, half] = regroup(tiles, y, group).astype(BF16)

    z = pl.multiple_of(place_ref[0] * 128, 128)
    y = place_ref[1]
    group = lane_group((PACKED, 128))
    for half in range(2):
        out = None
        for slot in range(4):
            tile = packed_ref[4 * half + slot, :, pl.ds(z, 128)].astype(F32)
            moved = pltpu.roll(tile, (SHARE * (slot - y)) & 127, 1)
            out = moved if out is None else jnp.where(group == slot, moved, out)
        own_ref[half] = out


def reduce_kernel(parts_ref, own_ref, grad_ref, cand_ref, total):
    total[...] = jnp.sum(parts_ref[...].astype(F32), axis=0)
    grad_ref[...] = jnp.zeros(grad_ref.shape, F32)
    grad_ref[:, :RB, :] = total[:, :RB, :]
    grad_ref[:, IM : IM + RB, :] = total[:, RB : 2 * RB, :]
    row = lax.broadcasted_iota(jnp.int32, cand_ref.shape, 1) % IM
    cand_ref[...] = jnp.where(row < RB, own_ref[...] - STEP * grad_ref[...], 0.0)


def shell_kernel(grad_ref, cand_ref, other_ref, out_ref, block):
    mine = cand_ref[...]
    other = other_ref[...]

    def shell(value):
        value = value[0] + value[1]
        return value[:IM] + value[IM:]

    sums = jnp.concatenate([shell(mine * other), shell(mine * mine), shell(other * other), jnp.zeros((IM, 128), F32)], axis=0)
    sums = jnp.sum(sums.T, axis=0, keepdims=True)
    group = lane_group((1, 128))
    block[...] = grad_ref[...]
    for item in range(3):
        row = None
        for slot in range(4):
            moved = pltpu.roll(sums, (IM * (slot - item)) % 128, 1)
            row = moved if row is None else jnp.where(group == slot, moved, row)
        high = row.astype(BF16).astype(F32)
        for half in range(2):
            block[half, RB + 2 * item : RB + 2 * item + 1, :] = high
            block[half, RB + 2 * item + 1 : RB + 2 * item + 2, :] = row - high
    group = lane_group((16, 128))
    for half in range(2):
        tiles = [block[half, 16 * fold : 16 * (fold + 1), :] for fold in range(4)]
        for slot in range(4):
            out_ref[4 * half + slot] = regroup(tiles, slot, group).astype(BF16)


def update_kernel(side_ref, map_ref, parts_ref, out_ref, scale):
    sums = jnp.zeros((N_SLAB, 16, 128), F32)
    for index in range(N_DOM):
        sums += parts_ref[index].astype(F32)
    first = RB - 16
    num = sums[:, first, :] + sums[:, first + 1, :]
    den_mine = sums[:, first + 2, :] + sums[:, first + 3, :]
    den_other = sums[:, first + 4, :] + sums[:, first + 5, :]
    fsc = num / (jnp.sqrt(den_mine * den_other) + 1e-06)
    factor = STEP * (1.0 + fsc) / 2.0
    factor = jnp.where(lane_group((N_SLAB, 128)) == 1, factor, 0.0)
    factor = jnp.concatenate([factor, jnp.zeros((128 - N_SLAB, 128), F32)], axis=0).T
    scale[...] = factor[SHARE : 2 * SHARE, :]
    group = lane_group((16, 128))

    @pl.loop(0, 8)
    def _(z):
        lanes = pl.ds(pl.multiple_of(z * 128, 128), 128)
        for part in range(N_SLAB):
            tiles = [parts_ref[4 * z + y, part].astype(F32) for y in range(4)]
            for fold in range(4):
                count = 16 if fold % 2 == 0 else RB - 16
                start = 16 * (fold % 2)
                at = R * (fold // 2) + RB * part + start
                value = regroup(tiles, fold, group)
                weight = scale[start : start + 16, part : part + 1]
                out_ref[at : at + count, lanes] = map_ref[at : at + count, lanes] - (weight * value)[:count]


def vmem():
    return pl.BlockSpec(memory_space=pltpu.VMEM)


def limit(mib):
    return pltpu.CompilerParams(vmem_limit_bytes=mib << 20)


def exchange(value, axis, side):
    flat = value.reshape(value.shape[0], -1, value.shape[-1])
    flat, side = lax.optimization_barrier((flat, side))
    moved = lax.all_to_all(flat, axis, 0, 0, tiled=True)
    moved, side = lax.optimization_barrier((moved, side * 0.5))
    return moved.reshape(value.shape), side


def line_terms(classes_local, shifts_local, defocus, radius):
    class_ids = jnp.arange(defocus.shape[0], dtype=jnp.int32)
    focus = jnp.sum(jnp.where(classes_local[:, None] == class_ids[None, :], defocus[None, :], 0.0), axis=1)
    ctf = -jnp.sin(CTF_GAIN * focus[None, :] * (radius[:, None] / R) ** 2 + PHASE_ZERO)
    ctf_rows = jnp.repeat(ctf, LPI, axis=1)
    theta = jnp.pi * jnp.arange(LPI, dtype=F32) / LPI
    theta_rows = jnp.tile(theta, classes_local.shape[0])
    shift_x = jnp.repeat(shifts_local[0].astype(F32), LPI)
    shift_y = jnp.repeat(shifts_local[1].astype(F32), LPI)
    along = shift_x * jnp.cos(theta_rows) + shift_y * jnp.sin(theta_rows)
    phase = 2.0 * jnp.pi * radius[:, None] * along[None, :] / (2.0 * R)
    return (ctf_rows, jnp.cos(phase), jnp.sin(phase))


def body(volume, images, tap_index, tap_weight, classes, shifts, defocus):
    map_t = volume[0].T
    data_t = images[0].T
    slab = lax.axis_index("slab")
    dom = lax.axis_index("dom")

    packed = pl.pallas_call(
        pack_kernel,
        out_shape=jax.ShapeDtypeStruct((N_SLAB, PACKED, LINES), BF16),
        in_specs=[vmem()] * 3,
        out_specs=vmem(),
        scratch_shapes=[pltpu.VMEM((PACKED, LINES), F32)],
        compiler_params=limit(6),
        name="pack",
    )(map_t, tap_index[0, 0], tap_weight[0, 0])
    packed, side = exchange(packed, "slab", defocus[:1])

    pad = ((0, IM - RB), (0, 0))
    radius = (RB * slab + jnp.arange(RB)).astype(F32)
    ctf, cosine, sine = line_terms(classes[0], shifts[0], defocus, radius)
    ctf, cosine, sine = (jnp.pad(ctf, pad), jnp.pad(cosine, pad), jnp.pad(sine, pad))
    data = lax.dynamic_slice(data_t.reshape(2, R, ROWS), (0, RB * slab, 0), (2, RB, ROWS))
    data = jnp.pad(data, ((0, 0),) + pad)
    place = jnp.stack([dom // 4, dom % 4]).astype(jnp.int32)

    parts, own = pl.pallas_call(
        image_kernel,
        out_shape=(
            jax.ShapeDtypeStruct((N_DOM, 2, TIGHT, 128), BF16),
            jax.ShapeDtypeStruct((2, PACKED, 128), F32),
        ),
        in_specs=[pl.BlockSpec(memory_space=pltpu.SMEM)] + [vmem()] * 5,
        out_specs=(vmem(), vmem()),
        scratch_shapes=[
            pltpu.VMEM((N_SLAB, LINES, ROWS), BF16),
            pltpu.VMEM((PACKED, ROWS), F32),
            pltpu.VMEM((TIGHT, ROWS), F32),
            pltpu.VMEM((N_SLAB, TIGHT, LINES), F32),
        ],
        compiler_params=limit(32),
        name="image",
    )(place, packed, data, ctf, cosine, sine)
    parts, side = exchange(parts, "dom", side)

    block = jax.ShapeDtypeStruct((2, PACKED, 128), F32)
    grad, cand = pl.pallas_call(
        reduce_kernel,
        out_shape=(block, block),
        in_specs=[vmem()] * 2,
        out_specs=(vmem(), vmem()),
        scratch_shapes=[pltpu.VMEM((2, TIGHT, 128), F32)],
        compiler_params=limit(4),
        name="reduce",
    )(parts, own)
    other = lax.ppermute(cand, "half", [(0, 1), (1, 0)])
    share = pl.pallas_call(
        shell_kernel,
        out_shape=jax.ShapeDtypeStruct((N_SLAB, 16, 128), BF16),
        in_specs=[vmem()] * 3,
        out_specs=vmem(),
        scratch_shapes=[pltpu.VMEM((2, PACKED, 128), F32)],
        compiler_params=limit(2),
        name="shell",
    )(grad, cand, other)
    share, side = exchange(share, "slab", side)
    every, side = exchange(jnp.broadcast_to(share[None], (N_DOM,) + share.shape), "dom", side)
    result = pl.pallas_call(
        update_kernel,
        out_shape=jax.ShapeDtypeStruct((2 * R, LINES), F32),
        in_specs=[pl.BlockSpec(memory_space=pltpu.SMEM)] + [vmem()] * 2,
        out_specs=vmem(),
        scratch_shapes=[pltpu.VMEM((SHARE, 128), F32)],
        compiler_params=limit(8),
        name="update",
    )(side, map_t, every)
    return result.T[None]


def solution(mesh):
    placed = (
        P("half", "slab", None),
        P("half", "dom", None),
        P("half", "slab", None, "dom"),
        P("half", "slab", None, "dom"),
        P("half", "dom"),
        P("half", None, "dom"),
        P(),
    )
    return jax.shard_map(
        body, mesh=mesh, in_specs=placed, out_specs=P("half", "slab", None), check_vma=False
    )
```

```python
import math

import jax
import jax.numpy as jnp
from jax import lax
from jax.experimental import pallas as pl
from jax.experimental.pallas import tpu as pltpu
from jax.sharding import PartitionSpec as P

LPI = 64
CTF_GAIN = 30.0
PHASE_ZERO = 0.1
STEP_SCALE = 0.5

R = 200
K = 8
N_SLAB = 8
N_X = 4
N_DOM = 32
LINES = 1024
ROWS = 1024
RB = R // N_X
SHARE = LINES // N_DOM
FOLD = RB // 2
STEP = STEP_SCALE / math.sqrt(ROWS * N_DOM * K / LINES)

F32 = jnp.float32
BF16 = jnp.bfloat16

IM = 56
BLOCK = 112
SENT = BLOCK + 8
TIGHT = 104
TAP_ROWS = (50, 51, 52, 53, 54, 55, 106, 107)
HIGH_ROW = 108
LOW_ROW = 109
SUM_ROWS = (50, 106)
CHUNK = 16


def lane_group(shape):
    return lax.broadcasted_iota(jnp.int32, shape, len(shape) - 1) // SHARE


def regroup(tiles, source, group):
    out = None
    for slot, tile in enumerate(tiles):
        moved = pltpu.roll(tile, (SHARE * (slot - source)) % 128, 1)
        out = moved if out is None else jnp.where(group == slot, moved, out)
    return out


def build_taps(taps, weights, high, low):
    line = lax.broadcasted_iota(jnp.int32, (CHUNK, ROWS), 0).astype(F32)
    first = jnp.zeros((CHUNK, ROWS), F32)
    second = jnp.zeros((CHUNK, ROWS), F32)
    for tap in range(K):
        first += jnp.where(line == low + tap, weights[tap], 0.0)
        second += jnp.where(line + CHUNK == low + tap, weights[tap], 0.0)
    first = first.astype(BF16)
    second = second.astype(BF16)
    high = jnp.broadcast_to(high, (CHUNK, ROWS)).astype(BF16)
    none = jnp.zeros((CHUNK, ROWS), BF16)
    before = None
    for chunk in range(LINES // CHUNK):
        here = high == jnp.asarray(chunk, BF16)
        value = jnp.where(here, first, none)
        if before is not None:
            value = jnp.where(before, second, value)
        taps[CHUNK * chunk : CHUNK * (chunk + 1), :] = value
        before = here


def project_kernel(place_ref, index_ref, weight_ref, map_hbm, out_ref, map_ref, block, taps, arrived):
    copy = pltpu.make_async_copy(map_hbm, map_ref, arrived)
    copy.start()
    index = index_ref[...]
    weight = weight_ref[...]
    base = jnp.min(index, axis=0, keepdims=True)
    place = lax.broadcasted_iota(jnp.int32, index.shape, 0)
    ordered = jnp.zeros(weight.shape, F32)
    for tap in range(K):
        ordered += jnp.where(place == index[tap : tap + 1] - base, weight[tap : tap + 1], 0.0)
    high = (base >> 4).astype(F32)
    low = (base & 15).astype(F32)
    weights = [ordered[tap : tap + 1] for tap in range(K)]
    build_taps(taps, weights, high, low)
    copy.wait()

    z = pl.multiple_of(place_ref[0] * 128, 128)
    y = place_ref[1]
    group = lane_group((8, 128))
    for part in range(N_X):
        at = BLOCK * part
        block[at + RB : at + IM, :] = jnp.zeros((IM - RB, LINES), F32)
        block[at + IM + RB : at + BLOCK, :] = jnp.zeros((IM - RB, LINES), F32)
        block[at : at + RB, :] = map_ref[RB * part : RB * (part + 1), :]
        block[at + IM : at + IM + RB, :] = map_ref[R + RB * part : R + RB * (part + 1), :]
        for lanes in range(LINES // 128):
            own = jnp.zeros((8, 128), F32)
            for slot in range(4):
                eight = 4 * lanes + slot
                if eight < BLOCK // 8:
                    tile = block[at + 8 * eight : at + 8 * eight + 8, pl.ds(z, 128)]
                    moved = pltpu.roll(tile, (SHARE * (slot - y)) & 127, 1)
                    own = jnp.where(group == slot, moved, own)
            out_ref[part, BLOCK:, 128 * lanes : 128 * (lanes + 1)] = own.astype(BF16)
    block[...] = jnp.dot(block[...].astype(BF16), taps[...], preferred_element_type=F32)
    for part in range(N_X):
        at = BLOCK * part
        for row, value in zip(TAP_ROWS + (HIGH_ROW, LOW_ROW), weights + [high, low], strict=True):
            block[at + row : at + row + 1, :] = value
        out_ref[part, :BLOCK, :] = block[at : at + BLOCK, :].astype(BF16)


def gather_kernel(parts_ref, mine_ref, low_ref, own_ref):
    total = parts_ref[0, :BLOCK].astype(F32)
    for part in range(1, N_X):
        total += parts_ref[part, :BLOCK].astype(F32)
    mine_ref[...] = total
    low_ref[...] = total.astype(BF16)
    group = lane_group((8, 128))
    for eight in range(BLOCK // 8):
        lanes = 128 * (eight // 4)
        tiles = [parts_ref[part, BLOCK:, lanes : lanes + 128].astype(F32) for part in range(N_X)]
        own_ref[8 * eight : 8 * eight + 8, :] = regroup(tiles, eight % 4, group)


def taps_kernel(parts_ref, taps_ref):
    @pl.loop(0, N_X)
    def _(part):
        rows = parts_ref[part].astype(F32)
        weights = [rows[row : row + 1] for row in TAP_ROWS]
        build_taps(taps_ref.at[part], weights, rows[HIGH_ROW : HIGH_ROW + 1], rows[LOW_ROW : LOW_ROW + 1])


def back_kernel(mine_ref, other_ref, data_ref, ctf_ref, cos_ref, sin_ref, taps_ref, out_ref, back, grad):
    ctf = ctf_ref[...]
    cosine = cos_ref[...]
    sine = sin_ref[...]
    proj = mine_ref[...] + other_ref[...].astype(F32)
    proj_re = proj[:IM]
    proj_im = proj[IM:]
    res_re = ctf * (cosine * proj_re - sine * proj_im) - data_ref[0].astype(F32)
    res_im = ctf * (sine * proj_re + cosine * proj_im) - data_ref[1].astype(F32)
    back_re = ctf * (cosine * res_re + sine * res_im)
    back_im = ctf * (cosine * res_im - sine * res_re)
    back[2 * RB :, :] = jnp.zeros((TIGHT - 2 * RB, ROWS), F32)
    back[:RB, :] = back_re[:RB]
    back[RB : 2 * RB, :] = back_im[:RB]
    back_low = back[...].astype(BF16)

    @pl.loop(0, N_X)
    def _(part):
        grad[part] = lax.dot_general(back_low, taps_ref[part], (((1,), (1,)), ((), ())), preferred_element_type=F32)

    group = lane_group((TIGHT, 128))
    for z in range(8):
        tiles = [grad[part, :, 128 * z : 128 * (z + 1)] for part in range(N_X)]
        for y in range(4):
            out_ref[4 * z + y] = regroup(tiles, y, group).astype(BF16)


def reduce_kernel(parts_ref, own_ref, grad_ref, cand_ref, total):
    total[...] = jnp.sum(parts_ref[...].astype(F32), axis=0)
    grad_ref[...] = jnp.zeros(grad_ref.shape, F32)
    grad_ref[:RB, :] = total[:RB, :]
    grad_ref[IM : IM + RB, :] = total[RB : 2 * RB, :]
    row = lax.broadcasted_iota(jnp.int32, cand_ref.shape, 0) % IM
    cand_ref[...] = jnp.where(row < RB, own_ref[...] - STEP * grad_ref[...], 0.0)


def split(value):
    high = value.astype(BF16).astype(F32)
    return high, value - high


def shell_kernel(grad_ref, cand_ref, other_ref, out_ref, block):
    mine = cand_ref[...]
    other = other_ref[...]
    for item, product in enumerate((mine * other, mine * mine, other * other)):
        shell = product[:IM] + product[IM:]
        shell = jnp.concatenate([shell, jnp.zeros((128 - IM, 128), F32)], axis=0)
        row = jnp.sum(shell.T, axis=0, keepdims=True)
        row = row + pltpu.roll(row, 64, 1)
        high, low = split(row)
        block[FOLD + 2 * item : FOLD + 2 * item + 1, :] = high
        block[FOLD + 2 * item + 1 : FOLD + 2 * item + 2, :] = low
    block[FOLD + 6 :, :] = jnp.zeros((32 - FOLD - 6, 128), F32)
    group = lane_group((FOLD, 128))
    tiles = [grad_ref[at : at + FOLD, :] for at in (0, FOLD, IM, IM + FOLD)]
    for slot in range(N_X):
        block[:FOLD, :] = regroup(tiles, slot, group)
        value = block[...].astype(BF16)
        out_ref[slot] = value
        out_ref[N_X + slot] = value


def share_kernel(place_ref, parts_ref, out_ref, block, whole, sent, left):
    first = place_ref[2] * N_X
    for part in range(N_X):
        block[part] = parts_ref[first + part].astype(F32)
    tiles = [block[part, :FOLD, :] for part in range(N_X)]
    group = lane_group((FOLD, 128))
    for fold, at in enumerate((0, FOLD, IM, IM + FOLD)):
        whole[at : at + FOLD, :] = regroup(tiles, fold, group)
    sums = []
    for part in range(N_X):
        block[part] = parts_ref[part].astype(F32) + parts_ref[N_X + part].astype(F32)
    lane = lax.broadcasted_iota(jnp.int32, (1, 128), 1)
    for pair, at in enumerate(SUM_ROWS):
        for item in range(3):
            row = FOLD + 2 * item
            sums = [block[2 * pair + side, row : row + 1, :] + block[2 * pair + side, row + 1 : row + 2, :] for side in (0, 1)]
            high, low = split(jnp.where(lane < 64, sums[0], sums[1]))
            whole[at + 2 * item : at + 2 * item + 1, :] = high
            whole[at + 2 * item + 1 : at + 2 * item + 2, :] = low
    sent[...] = whole[...].astype(BF16)
    copies = [pltpu.make_async_copy(sent, out_ref.at[dom], left.at[dom]) for dom in range(N_DOM)]
    for copy in copies:
        copy.start()
    for copy in copies:
        copy.wait()


def update_kernel(side_ref, map_ref, parts_ref, out_ref, sums, scale):
    total = parts_ref[0].astype(F32)
    for dom in range(1, N_DOM):
        total += parts_ref[dom].astype(F32)
    sums[...] = total
    factors = []
    for at in SUM_ROWS:
        num, den_mine, den_other = [sums[row : row + 1, :] + sums[row + 1 : row + 2, :] for row in (at, at + 2, at + 4)]
        fsc = num / (jnp.sqrt(den_mine * den_other) + 1e-06)
        factors.append(STEP * (1.0 + fsc) / 2.0)
    factors.append(jnp.zeros((128 - len(factors), 128), F32))
    scale[...] = jnp.concatenate(factors, axis=0).T
    group = lane_group((BLOCK, 128))

    @pl.loop(0, 8)
    def _(z):
        lanes = pl.ds(pl.multiple_of(z * 128, 128), 128)
        tiles = [parts_ref[4 * z + y].astype(F32) for y in range(4)]
        for part in range(N_X):
            value = regroup(tiles, part, group)
            side = 64 * (part % 2)
            weight = scale[side : side + IM, part // 2 : part // 2 + 1]
            for at, rows in ((RB * part, value[:IM]), (R + RB * part, value[IM:])):
                out_ref[at : at + RB, lanes] = map_ref[at : at + RB, lanes] - (weight * rows)[:RB]


def vmem():
    return pl.BlockSpec(memory_space=pltpu.VMEM)


def smem():
    return pl.BlockSpec(memory_space=pltpu.SMEM)


def limit(mib):
    return pltpu.CompilerParams(vmem_limit_bytes=mib << 20)


def cost(flops, moved):
    return pl.CostEstimate(flops=flops, bytes_accessed=moved, transcendentals=0)


def exchange(value, axis, side, groups=None):
    value, side = lax.optimization_barrier((value, side))
    moved = lax.all_to_all(value, axis, 0, 0, tiled=True, axis_index_groups=groups)
    return lax.optimization_barrier((moved, side * 0.5))


def line_terms(classes_local, shifts_local, defocus, radius):
    class_ids = jnp.arange(defocus.shape[0], dtype=jnp.int32)
    focus = jnp.sum(jnp.where(classes_local[:, None] == class_ids[None, :], defocus[None, :], 0.0), axis=1)
    ctf = -jnp.sin(CTF_GAIN * focus[None, :] * (radius[:, None] / R) ** 2 + PHASE_ZERO)
    ctf_rows = jnp.repeat(ctf, LPI, axis=1)
    theta = jnp.pi * jnp.arange(LPI, dtype=F32) / LPI
    theta_rows = jnp.tile(theta, classes_local.shape[0])
    shift_x = jnp.repeat(shifts_local[0].astype(F32), LPI)
    shift_y = jnp.repeat(shifts_local[1].astype(F32), LPI)
    along = shift_x * jnp.cos(theta_rows) + shift_y * jnp.sin(theta_rows)
    phase = 2.0 * jnp.pi * radius[:, None] * along[None, :] / (2.0 * R)
    return (ctf_rows, jnp.cos(phase), jnp.sin(phase))


def body(volume, images, tap_index, tap_weight, classes, shifts, defocus):
    map_t = volume[0].T
    data_t = images[0].T
    slab = lax.axis_index("slab")
    dom = lax.axis_index("dom")
    x = slab & 3
    place = jnp.stack([dom >> 2, dom & 3, slab >> 2]).astype(jnp.int32)
    runs = [[N_X * run + at for at in range(N_X)] for run in range(N_SLAB // N_X)]

    sent = jax.ShapeDtypeStruct((N_X, SENT, ROWS), BF16)
    parts = pl.pallas_call(
        project_kernel,
        out_shape=sent,
        in_specs=[smem(), vmem(), vmem(), pl.BlockSpec(memory_space=pl.ANY)],
        out_specs=vmem(),
        scratch_shapes=[
            pltpu.VMEM((2 * R, LINES), F32),
            pltpu.VMEM((N_X * BLOCK, LINES), F32),
            pltpu.VMEM((LINES, ROWS), BF16),
            pltpu.SemaphoreType.DMA(()),
        ],
        name="project",
    )(place, tap_index[0, 0], tap_weight[0, 0], map_t)
    parts, side = exchange(parts, "slab", defocus[:1], runs)

    pad = ((0, IM - RB), (0, 0))
    radius = (RB * x + jnp.arange(RB)).astype(F32)
    ctf, cosine, sine = line_terms(classes[0], shifts[0], defocus, radius)
    ctf, cosine, sine = (jnp.pad(ctf, pad), jnp.pad(cosine, pad), jnp.pad(sine, pad))
    data = lax.dynamic_slice(data_t.reshape(2, R, ROWS), (0, RB * x, 0), (2, RB, ROWS))
    data = jnp.pad(data, ((0, 0),) + pad)

    shard = jax.ShapeDtypeStruct((BLOCK, 128), F32)
    mine, low, own = pl.pallas_call(
        gather_kernel,
        out_shape=(
            jax.ShapeDtypeStruct((BLOCK, ROWS), F32),
            jax.ShapeDtypeStruct((BLOCK, ROWS), BF16),
            shard,
        ),
        in_specs=[vmem()],
        out_specs=(vmem(), vmem(), vmem()),
        compiler_params=limit(4),
        name="gather",
    )(parts)
    other = lax.ppermute(low, "slab", [(at, at ^ N_X) for at in range(N_SLAB)])
    taps = pl.pallas_call(
        taps_kernel,
        out_shape=jax.ShapeDtypeStruct((N_X, LINES, ROWS), BF16),
        in_specs=[vmem()],
        out_specs=vmem(),
        compiler_params=limit(16),
        cost_estimate=cost(1 << 24, 10 << 20),
        name="taps",
    )(parts)
    parts = pl.pallas_call(
        back_kernel,
        out_shape=jax.ShapeDtypeStruct((N_DOM, TIGHT, 128), BF16),
        in_specs=[vmem()] * 7,
        out_specs=vmem(),
        scratch_shapes=[
            pltpu.VMEM((TIGHT, ROWS), F32),
            pltpu.VMEM((N_X, TIGHT, LINES), F32),
        ],
        compiler_params=limit(16),
        name="back",
    )(mine, other, data, ctf, cosine, sine, taps)
    parts, side = exchange(parts, "dom", side)

    grad, cand = pl.pallas_call(
        reduce_kernel,
        out_shape=(shard, shard),
        in_specs=[vmem()] * 2,
        out_specs=(vmem(), vmem()),
        scratch_shapes=[pltpu.VMEM((TIGHT, 128), F32)],
        compiler_params=limit(4),
        name="reduce",
    )(parts, own)
    other = lax.ppermute(cand, "half", [(0, 1), (1, 0)])
    share = pl.pallas_call(
        shell_kernel,
        out_shape=jax.ShapeDtypeStruct((N_SLAB, 32, 128), BF16),
        in_specs=[vmem()] * 3,
        out_specs=vmem(),
        scratch_shapes=[pltpu.VMEM((32, 128), F32)],
        compiler_params=limit(2),
        name="shell",
    )(grad, cand, other)
    share, side = exchange(share, "slab", side)
    every = pl.pallas_call(
        share_kernel,
        out_shape=jax.ShapeDtypeStruct((N_DOM, BLOCK, 128), BF16),
        in_specs=[smem(), vmem()],
        out_specs=pl.BlockSpec(memory_space=pltpu.HBM),
        scratch_shapes=[
            pltpu.VMEM((N_X, 32, 128), F32),
            pltpu.VMEM((BLOCK, 128), F32),
            pltpu.VMEM((BLOCK, 128), BF16),
            pltpu.SemaphoreType.DMA((N_DOM,)),
        ],
        compiler_params=limit(4),
        name="share",
    )(place, share)
    every, side = exchange(every, "dom", side)
    result = pl.pallas_call(
        update_kernel,
        out_shape=jax.ShapeDtypeStruct((2 * R, LINES), F32),
        in_specs=[smem(), vmem(), vmem()],
        out_specs=vmem(),
        scratch_shapes=[pltpu.VMEM((BLOCK, 128), F32), pltpu.VMEM((128, 128), F32)],
        compiler_params=limit(8),
        name="update",
    )(side, map_t, every)
    return result.T[None]


def solution(mesh):
    placed = (
        P("half", "slab", None),
        P("half", "dom", None),
        P("half", "slab", None, "dom"),
        P("half", "slab", None, "dom"),
        P("half", "dom"),
        P("half", None, "dom"),
        P(),
    )
    return jax.shard_map(
        body, mesh=mesh, in_specs=placed, out_specs=P("half", "slab", None), check_vma=False
    )
```

```python
import math

import jax
import jax.numpy as jnp
from jax import lax
from jax.experimental import pallas as pl
from jax.experimental.pallas import tpu as pltpu
from jax.sharding import PartitionSpec as P

LPI = 64
CTF_GAIN = 30.0
PHASE_ZERO = 0.1
STEP_SCALE = 0.5

R = 200
K = 8
N_SLAB = 8
N_X = 4
N_DOM = 32
LINES = 1024
ROWS = 1024
RB = R // N_X
SHARE = LINES // N_DOM
FOLD = RB // 2
STEP = STEP_SCALE / math.sqrt(ROWS * N_DOM * K / LINES)

F32 = jnp.float32
BF16 = jnp.bfloat16

IM = 56
BLOCK = 112
SENT = BLOCK + 8
TIGHT = 104
TAP_ROWS = (50, 51, 52, 53, 54, 55, 106, 107)
HIGH_ROW = 108
LOW_ROW = 109
SUM_ROWS = (50, 106)
CHUNK = 16


def lane_group(shape):
    return lax.broadcasted_iota(jnp.int32, shape, len(shape) - 1) // SHARE


def regroup(tiles, source, group):
    out = None
    for slot, tile in enumerate(tiles):
        moved = pltpu.roll(tile, (SHARE * (slot - source)) % 128, 1)
        out = moved if out is None else jnp.where(group == slot, moved, out)
    return out


def regroup_all(tiles, group):
    low = group < 2
    even = (group & 1) == 0
    half = [jnp.where(low, tiles[at], pltpu.roll(tiles[at + 2], 2 * SHARE, 1)) for at in range(2)]
    half += [jnp.where(low, pltpu.roll(tiles[at], 2 * SHARE, 1), tiles[at + 2]) for at in range(2)]
    out = []
    for at in (0, 2):
        out.append(jnp.where(even, half[at], pltpu.roll(half[at + 1], SHARE, 1)))
        out.append(jnp.where(even, pltpu.roll(half[at], 3 * SHARE, 1), half[at + 1]))
    return out


def build_taps(taps, weights, high, low):
    line = lax.broadcasted_iota(jnp.int32, (CHUNK, ROWS), 0).astype(F32)
    first = jnp.zeros((CHUNK, ROWS), F32)
    second = jnp.zeros((CHUNK, ROWS), F32)
    for tap in range(K):
        first += jnp.where(line == low + tap, weights[tap], 0.0)
        second += jnp.where(line + CHUNK == low + tap, weights[tap], 0.0)
    first = first.astype(BF16)
    second = second.astype(BF16)
    high = jnp.broadcast_to(high, (CHUNK, ROWS)).astype(BF16)
    none = jnp.zeros((CHUNK, ROWS), BF16)
    before = None
    for chunk in range(LINES // CHUNK):
        here = high == jnp.asarray(chunk, BF16)
        value = jnp.where(here, first, none)
        if before is not None:
            value = jnp.where(before, second, value)
        taps[CHUNK * chunk : CHUNK * (chunk + 1), :] = value
        before = here


def project_kernel(index_ref, weight_ref, map_hbm, out_ref, map_ref, block, taps, arrived):
    copy = pltpu.make_async_copy(map_hbm, map_ref, arrived)
    copy.start()
    index = index_ref[...]
    weight = weight_ref[...]
    base = jnp.min(index, axis=0, keepdims=True)
    place = lax.broadcasted_iota(jnp.int32, index.shape, 0)
    ordered = jnp.zeros(weight.shape, F32)
    for tap in range(K):
        ordered += jnp.where(place == index[tap : tap + 1] - base, weight[tap : tap + 1], 0.0)
    high = (base >> 4).astype(F32)
    low = (base & 15).astype(F32)
    weights = [ordered[tap : tap + 1] for tap in range(K)]
    build_taps(taps, weights, high, low)
    copy.wait()

    dom = lax.axis_index("dom")
    z = pl.multiple_of((dom >> 2) * 128, 128)
    y = dom & 3
    group = lane_group((8, 128))
    for part in range(N_X):
        at = BLOCK * part
        block[at + RB : at + IM, :] = jnp.zeros((IM - RB, LINES), F32)
        block[at + IM + RB : at + BLOCK, :] = jnp.zeros((IM - RB, LINES), F32)
        block[at : at + RB, :] = map_ref[RB * part : RB * (part + 1), :]
        block[at + IM : at + IM + RB, :] = map_ref[R + RB * part : R + RB * (part + 1), :]
        for lanes in range(LINES // 128):
            own = jnp.zeros((8, 128), F32)
            for slot in range(4):
                eight = 4 * lanes + slot
                if eight < BLOCK // 8:
                    tile = block[at + 8 * eight : at + 8 * eight + 8, pl.ds(z, 128)]
                    moved = pltpu.roll(tile, (SHARE * (slot - y)) & 127, 1)
                    own = jnp.where(group == slot, moved, own)
            out_ref[part, BLOCK:, 128 * lanes : 128 * (lanes + 1)] = own.astype(BF16)
    block[...] = jnp.dot(block[...].astype(BF16), taps[...], preferred_element_type=F32)
    for part in range(N_X):
        at = BLOCK * part
        for row, value in zip(TAP_ROWS + (HIGH_ROW, LOW_ROW), weights + [high, low], strict=True):
            block[at + row : at + row + 1, :] = value
        out_ref[part, :BLOCK, :] = block[at : at + BLOCK, :].astype(BF16)


def gather_kernel(parts_ref, mine_ref, low_ref, own_ref):
    total = parts_ref[0, :BLOCK].astype(F32)
    for part in range(1, N_X):
        total += parts_ref[part, :BLOCK].astype(F32)
    mine_ref[...] = total
    low_ref[...] = total.astype(BF16)
    group = lane_group((8, 128))
    for eight in range(BLOCK // 8):
        lanes = 128 * (eight // 4)
        tiles = [parts_ref[part, BLOCK:, lanes : lanes + 128].astype(F32) for part in range(N_X)]
        own_ref[8 * eight : 8 * eight + 8, :] = regroup(tiles, eight % 4, group)


def taps_kernel(parts_ref, taps_ref):
    @pl.loop(0, N_X)
    def _(part):
        rows = parts_ref[part].astype(F32)
        weights = [rows[row : row + 1] for row in TAP_ROWS]
        build_taps(taps_ref.at[part], weights, rows[HIGH_ROW : HIGH_ROW + 1], rows[LOW_ROW : LOW_ROW + 1])


def back_kernel(mine_ref, other_ref, data_ref, ctf_ref, cos_ref, sin_ref, taps_ref, out_ref, back, grad):
    ctf = ctf_ref[...]
    cosine = cos_ref[...]
    sine = sin_ref[...]
    proj = mine_ref[...] + other_ref[...].astype(F32)
    proj_re = proj[:IM]
    proj_im = proj[IM:]
    res_re = ctf * (cosine * proj_re - sine * proj_im) - data_ref[0].astype(F32)
    res_im = ctf * (sine * proj_re + cosine * proj_im) - data_ref[1].astype(F32)
    back_re = ctf * (cosine * res_re + sine * res_im)
    back_im = ctf * (cosine * res_im - sine * res_re)
    back[2 * RB :, :] = jnp.zeros((TIGHT - 2 * RB, ROWS), F32)
    back[:RB, :] = back_re[:RB]
    back[RB : 2 * RB, :] = back_im[:RB]
    back_low = back[...].astype(BF16)

    for part in range(N_X):
        grad[part] = lax.dot_general(back_low, taps_ref[part], (((1,), (1,)), ((), ())), preferred_element_type=F32)

    group = lane_group((TIGHT, 128))
    for z in range(8):
        tiles = [grad[part, :, 128 * z : 128 * (z + 1)] for part in range(N_X)]
        for y, value in enumerate(regroup_all(tiles, group)):
            out_ref[4 * z + y] = value.astype(BF16)


def reduce_kernel(parts_ref, own_ref, grad_ref, cand_ref, total):
    total[...] = jnp.sum(parts_ref[...].astype(F32), axis=0)
    grad_ref[...] = jnp.zeros(grad_ref.shape, F32)
    grad_ref[:RB, :] = total[:RB, :]
    grad_ref[IM : IM + RB, :] = total[RB : 2 * RB, :]
    row = lax.broadcasted_iota(jnp.int32, cand_ref.shape, 0) % IM
    cand_ref[...] = jnp.where(row < RB, own_ref[...] - STEP * grad_ref[...], 0.0)


def split(value):
    high = value.astype(BF16).astype(F32)
    return high, value - high


def shell_kernel(grad_ref, cand_ref, other_ref, out_ref, block):
    mine = cand_ref[...]
    other = other_ref[...]
    for item, product in enumerate((mine * other, mine * mine, other * other)):
        shell = product[:IM] + product[IM:]
        shell = jnp.concatenate([shell, jnp.zeros((128 - IM, 128), F32)], axis=0)
        row = jnp.sum(shell.T, axis=0, keepdims=True)
        row = row + pltpu.roll(row, 64, 1)
        high, low = split(row)
        block[FOLD + 2 * item : FOLD + 2 * item + 1, :] = high
        block[FOLD + 2 * item + 1 : FOLD + 2 * item + 2, :] = low
    block[FOLD + 6 :, :] = jnp.zeros((32 - FOLD - 6, 128), F32)
    group = lane_group((FOLD, 128))
    tiles = [grad_ref[at : at + FOLD, :] for at in (0, FOLD, IM, IM + FOLD)]
    for slot, folded in enumerate(regroup_all(tiles, group)):
        block[:FOLD, :] = folded
        value = block[...].astype(BF16)
        out_ref[slot] = value
        out_ref[N_X + slot] = value


def share_kernel(parts_ref, out_ref, block, whole):
    first = (lax.axis_index("slab") >> 2) * N_X
    for part in range(N_X):
        block[part] = parts_ref[first + part].astype(F32)
    tiles = [block[part, :FOLD, :] for part in range(N_X)]
    group = lane_group((FOLD, 128))
    for at, value in zip((0, FOLD, IM, IM + FOLD), regroup_all(tiles, group), strict=True):
        whole[at : at + FOLD, :] = value
    for part in range(N_X):
        block[part] = parts_ref[part].astype(F32) + parts_ref[N_X + part].astype(F32)
    lane = lax.broadcasted_iota(jnp.int32, (1, 128), 1)
    for pair, at in enumerate(SUM_ROWS):
        for item in range(3):
            row = FOLD + 2 * item
            sums = [block[2 * pair + side, row : row + 1, :] + block[2 * pair + side, row + 1 : row + 2, :] for side in (0, 1)]
            high, low = split(jnp.where(lane < 64, sums[0], sums[1]))
            whole[at + 2 * item : at + 2 * item + 1, :] = high
            whole[at + 2 * item + 1 : at + 2 * item + 2, :] = low
    value = whole[...].astype(BF16)
    for dom in range(N_DOM):
        out_ref[dom] = value


def update_kernel(map_ref, parts_ref, out_hbm, out_ref, sums, scale, left):
    total = parts_ref[0].astype(F32)
    for dom in range(1, N_DOM):
        total += parts_ref[dom].astype(F32)
    sums[...] = total
    factors = []
    for at in SUM_ROWS:
        num, den_mine, den_other = [sums[row : row + 1, :] + sums[row + 1 : row + 2, :] for row in (at, at + 2, at + 4)]
        fsc = num / (jnp.sqrt(den_mine * den_other) + 1e-06)
        factors.append(STEP * (1.0 + fsc) / 2.0)
    factors.append(jnp.zeros((128 - len(factors), 128), F32))
    scale[...] = jnp.concatenate(factors, axis=0).T
    group = lane_group((BLOCK, 128))

    def copy(z):
        lanes = pl.ds(pl.multiple_of(z * 128, 128), 128)
        return pltpu.make_async_copy(out_ref.at[:, lanes], out_hbm.at[:, lanes], left.at[z])

    @pl.loop(0, 8)
    def _(z):
        lanes = pl.ds(pl.multiple_of(z * 128, 128), 128)
        tiles = [parts_ref[4 * z + y].astype(F32) for y in range(4)]
        for part, value in enumerate(regroup_all(tiles, group)):
            side = 64 * (part % 2)
            weight = scale[side : side + IM, part // 2 : part // 2 + 1]
            for at, rows in ((RB * part, value[:IM]), (R + RB * part, value[IM:])):
                out_ref[at : at + RB, lanes] = map_ref[at : at + RB, lanes] - (weight * rows)[:RB]
        copy(z).start()

    for z in range(8):
        copy(z).wait()


def vmem():
    return pl.BlockSpec(memory_space=pltpu.VMEM)


def limit(mib):
    return pltpu.CompilerParams(vmem_limit_bytes=mib << 20)


def cost(flops, moved):
    return pl.CostEstimate(flops=flops, bytes_accessed=moved, transcendentals=0)


def exchange(value, axis, groups=None):
    return lax.all_to_all(value, axis, 0, 0, tiled=True, axis_index_groups=groups)


def line_terms(classes_local, shifts_local, defocus, radius):
    class_ids = jnp.arange(defocus.shape[0], dtype=jnp.int32)
    focus = jnp.sum(jnp.where(classes_local[:, None] == class_ids[None, :], defocus[None, :], 0.0), axis=1)
    ctf = -jnp.sin(CTF_GAIN * focus[None, :] * (radius[:, None] / R) ** 2 + PHASE_ZERO)
    ctf_rows = jnp.repeat(ctf, LPI, axis=1)
    theta = jnp.pi * jnp.arange(LPI, dtype=F32) / LPI
    theta_rows = jnp.tile(theta, classes_local.shape[0])
    shift_x = jnp.repeat(shifts_local[0].astype(F32), LPI)
    shift_y = jnp.repeat(shifts_local[1].astype(F32), LPI)
    along = shift_x * jnp.cos(theta_rows) + shift_y * jnp.sin(theta_rows)
    phase = 2.0 * jnp.pi * radius[:, None] * along[None, :] / (2.0 * R)
    return (ctf_rows, jnp.cos(phase), jnp.sin(phase))


def body(volume, images, tap_index, tap_weight, classes, shifts, defocus):
    map_t = volume[0].T
    data_t = images[0].T
    slab = lax.axis_index("slab")
    x = slab & 3
    runs = [[N_X * run + at for at in range(N_X)] for run in range(N_SLAB // N_X)]

    sent = jax.ShapeDtypeStruct((N_X, SENT, ROWS), BF16)
    parts = pl.pallas_call(
        project_kernel,
        out_shape=sent,
        in_specs=[vmem(), vmem(), pl.BlockSpec(memory_space=pl.ANY)],
        out_specs=vmem(),
        scratch_shapes=[
            pltpu.VMEM((2 * R, LINES), F32),
            pltpu.VMEM((N_X * BLOCK, LINES), F32),
            pltpu.VMEM((LINES, ROWS), BF16),
            pltpu.SemaphoreType.DMA(()),
        ],
        name="project",
    )(tap_index[0, 0], tap_weight[0, 0], map_t)
    parts = exchange(parts, "slab", runs)

    pad = ((0, IM - RB), (0, 0))
    radius = (RB * x + jnp.arange(RB)).astype(F32)
    ctf, cosine, sine = line_terms(classes[0], shifts[0], defocus, radius)
    ctf, cosine, sine = (jnp.pad(ctf, pad), jnp.pad(cosine, pad), jnp.pad(sine, pad))
    data = lax.dynamic_slice(data_t.reshape(2, R, ROWS), (0, RB * x, 0), (2, RB, ROWS))
    data = jnp.pad(data, ((0, 0),) + pad)
    parts, ctf, cosine, sine, data = lax.optimization_barrier((parts, ctf, cosine, sine, data))

    shard = jax.ShapeDtypeStruct((BLOCK, 128), F32)
    mine, low, own = pl.pallas_call(
        gather_kernel,
        out_shape=(
            jax.ShapeDtypeStruct((BLOCK, ROWS), F32),
            jax.ShapeDtypeStruct((BLOCK, ROWS), BF16),
            shard,
        ),
        in_specs=[vmem()],
        out_specs=(vmem(), vmem(), vmem()),
        compiler_params=limit(4),
        name="gather",
    )(parts)
    other = lax.ppermute(low, "slab", [(at, at ^ N_X) for at in range(N_SLAB)])
    taps = pl.pallas_call(
        taps_kernel,
        out_shape=jax.ShapeDtypeStruct((N_X, LINES, ROWS), BF16),
        in_specs=[vmem()],
        out_specs=vmem(),
        compiler_params=limit(16),
        cost_estimate=cost(1 << 24, 10 << 20),
        name="taps",
    )(parts)
    parts = pl.pallas_call(
        back_kernel,
        out_shape=jax.ShapeDtypeStruct((N_DOM, TIGHT, 128), BF16),
        in_specs=[vmem()] * 7,
        out_specs=vmem(),
        scratch_shapes=[
            pltpu.VMEM((TIGHT, ROWS), F32),
            pltpu.VMEM((N_X, TIGHT, LINES), F32),
        ],
        compiler_params=limit(16),
        name="back",
    )(mine, other, data, ctf, cosine, sine, taps)
    parts = exchange(parts, "dom")

    grad, cand = pl.pallas_call(
        reduce_kernel,
        out_shape=(shard, shard),
        in_specs=[vmem()] * 2,
        out_specs=(vmem(), vmem()),
        scratch_shapes=[pltpu.VMEM((TIGHT, 128), F32)],
        compiler_params=limit(4),
        name="reduce",
    )(parts, own)
    other = lax.ppermute(cand, "half", [(0, 1), (1, 0)])
    share = pl.pallas_call(
        shell_kernel,
        out_shape=jax.ShapeDtypeStruct((N_SLAB, 32, 128), BF16),
        in_specs=[vmem()] * 3,
        out_specs=vmem(),
        scratch_shapes=[pltpu.VMEM((32, 128), F32)],
        compiler_params=limit(2),
        name="shell",
    )(grad, cand, other)
    share = exchange(share, "slab")
    every = pl.pallas_call(
        share_kernel,
        out_shape=jax.ShapeDtypeStruct((N_DOM, BLOCK, 128), BF16),
        in_specs=[vmem()],
        out_specs=vmem(),
        scratch_shapes=[pltpu.VMEM((N_X, 32, 128), F32), pltpu.VMEM((BLOCK, 128), F32)],
        compiler_params=limit(4),
        name="share",
    )(share)
    every = exchange(every, "dom")
    result = pl.pallas_call(
        update_kernel,
        out_shape=jax.ShapeDtypeStruct((2 * R, LINES), F32),
        in_specs=[vmem(), vmem()],
        out_specs=pl.BlockSpec(memory_space=pl.ANY),
        scratch_shapes=[
            pltpu.VMEM((2 * R, LINES), F32),
            pltpu.VMEM((BLOCK, 128), F32),
            pltpu.VMEM((128, 128), F32),
            pltpu.SemaphoreType.DMA((8,)),
        ],
        compiler_params=limit(8),
        name="update",
    )(map_t, every)
    return result.T[None]


def solution(mesh):
    placed = (
        P("half", "slab", None),
        P("half", "dom", None),
        P("half", "slab", None, "dom"),
        P("half", "slab", None, "dom"),
        P("half", "dom"),
        P("half", None, "dom"),
        P(),
    )
    return jax.shard_map(
        body, mesh=mesh, in_specs=placed, out_specs=P("half", "slab", None), check_vma=False
    )
```

```python
import math

import jax
import jax.numpy as jnp
from jax import lax
from jax.experimental import pallas as pl
from jax.experimental.pallas import tpu as pltpu
from jax.sharding import PartitionSpec as P

LPI = 64
CTF_GAIN = 30.0
PHASE_ZERO = 0.1
STEP_SCALE = 0.5

R = 200
K = 8
N_SLAB = 8
N_X = 4
N_DOM = 32
LINES = 1024
ROWS = 1024
RB = R // N_X
SHARE = LINES // N_DOM
FOLD = RB // 2
STEP = STEP_SCALE / math.sqrt(ROWS * N_DOM * K / LINES)

F32 = jnp.float32
BF16 = jnp.bfloat16

IM = 56
BLOCK = 112
SENT = BLOCK + 8
TIGHT = 104
TAP_ROWS = (50, 51, 52, 53, 54, 55, 106, 107)
HIGH_ROW = 108
LOW_ROW = 109
SUM_ROWS = (50, 106)
SUM_TILES = (48, 96)
CHUNK = 16
PIECES = (0, 56, 104, 152, 200, 256, 304, 352, 400)


def lane_group(shape):
    return lax.broadcasted_iota(jnp.int32, shape, len(shape) - 1) // SHARE


def regroup(tiles, source, group):
    out = None
    for slot, tile in enumerate(tiles):
        moved = pltpu.roll(tile, (SHARE * (slot - source)) % 128, 1)
        out = moved if out is None else jnp.where(group == slot, moved, out)
    return out


def regroup_all(tiles, group):
    low = group < 2
    even = (group & 1) == 0
    half = [jnp.where(low, tiles[at], pltpu.roll(tiles[at + 2], 2 * SHARE, 1)) for at in range(2)]
    half += [jnp.where(low, pltpu.roll(tiles[at], 2 * SHARE, 1), tiles[at + 2]) for at in range(2)]
    out = []
    for at in (0, 2):
        out.append(jnp.where(even, half[at], pltpu.roll(half[at + 1], SHARE, 1)))
        out.append(jnp.where(even, pltpu.roll(half[at], 3 * SHARE, 1), half[at + 1]))
    return out


def build_taps(taps, weights, high, low):
    line = lax.broadcasted_iota(jnp.int32, (CHUNK, ROWS), 0).astype(F32)
    first = jnp.zeros((CHUNK, ROWS), F32)
    second = jnp.zeros((CHUNK, ROWS), F32)
    for tap in range(K):
        first += jnp.where(line == low + tap, weights[tap], 0.0)
        second += jnp.where(line + CHUNK == low + tap, weights[tap], 0.0)
    first = first.astype(BF16)
    second = second.astype(BF16)
    high = jnp.broadcast_to(high, (CHUNK, ROWS)).astype(BF16)
    none = jnp.zeros((CHUNK, ROWS), BF16)
    before = None
    for chunk in range(LINES // CHUNK):
        here = high == jnp.asarray(chunk, BF16)
        value = jnp.where(here, first, none)
        if before is not None:
            value = jnp.where(before, second, value)
        taps[CHUNK * chunk : CHUNK * (chunk + 1), :] = value
        before = here


def project_kernel(index_ref, weight_ref, map_hbm, out_hbm, map_ref, block, taps, out_ref, arrived, left):
    pieces = []
    for piece in range(2 * N_X):
        rows = slice(PIECES[piece], PIECES[piece + 1])
        pieces.append(pltpu.make_async_copy(map_hbm.at[rows], map_ref.at[rows], arrived.at[piece]))
    for part in range(N_X):
        pieces[part].start()
        pieces[N_X + part].start()
    index = index_ref[...]
    weight = weight_ref[...]
    base = jnp.min(index, axis=0, keepdims=True)
    place = lax.broadcasted_iota(jnp.int32, index.shape, 0)
    ordered = jnp.zeros(weight.shape, F32)
    for tap in range(K):
        ordered += jnp.where(place == index[tap : tap + 1] - base, weight[tap : tap + 1], 0.0)
    high = (base >> 4).astype(F32)
    low = (base & 15).astype(F32)
    weights = [ordered[tap : tap + 1] for tap in range(K)]
    build_taps(taps, weights, high, low)

    dom = lax.axis_index("dom")
    z = pl.multiple_of((dom >> 2) * 128, 128)
    y = dom & 3
    group = lane_group((8, 128))
    for part in range(N_X):
        at = BLOCK * part
        pieces[part].wait()
        pieces[N_X + part].wait()
        block[at + RB : at + IM, :] = jnp.zeros((IM - RB, LINES), F32)
        block[at + IM + RB : at + BLOCK, :] = jnp.zeros((IM - RB, LINES), F32)
        block[at : at + RB, :] = map_ref[RB * part : RB * (part + 1), :]
        block[at + IM : at + IM + RB, :] = map_ref[R + RB * part : R + RB * (part + 1), :]
        for lanes in range(LINES // 128):
            own = jnp.zeros((8, 128), F32)
            for slot in range(4):
                eight = 4 * lanes + slot
                if eight < BLOCK // 8:
                    tile = block[at + 8 * eight : at + 8 * eight + 8, pl.ds(z, 128)]
                    moved = pltpu.roll(tile, (SHARE * (slot - y)) & 127, 1)
                    own = jnp.where(group == slot, moved, own)
            out_ref[part, BLOCK:, 128 * lanes : 128 * (lanes + 1)] = own.astype(BF16)
    block[...] = jnp.dot(block[...].astype(BF16), taps[...], preferred_element_type=F32)
    for part in range(N_X):
        at = BLOCK * part
        for row, value in zip(TAP_ROWS + (HIGH_ROW, LOW_ROW), weights + [high, low], strict=True):
            block[at + row : at + row + 1, :] = value
        out_ref[part, :BLOCK, :] = block[at : at + BLOCK, :].astype(BF16)
        pltpu.make_async_copy(out_ref.at[part], out_hbm.at[part], left.at[part]).start()
    for part in range(N_X):
        pltpu.make_async_copy(out_ref.at[part], out_hbm.at[part], left.at[part]).wait()


def gather_kernel(parts_ref, mine_ref, low_ref, own_ref):
    total = parts_ref[0, :BLOCK].astype(F32)
    for part in range(1, N_X):
        total += parts_ref[part, :BLOCK].astype(F32)
    mine_ref[...] = total
    low_ref[...] = total.astype(BF16)
    group = lane_group((8, 128))
    for eight in range(BLOCK // 8):
        lanes = 128 * (eight // 4)
        tiles = [parts_ref[part, BLOCK:, lanes : lanes + 128].astype(F32) for part in range(N_X)]
        own_ref[8 * eight : 8 * eight + 8, :] = regroup(tiles, eight % 4, group)


def taps_kernel(parts_ref, taps_ref):
    @pl.loop(0, N_X)
    def _(part):
        rows = parts_ref[part].astype(F32)
        weights = [rows[row : row + 1] for row in TAP_ROWS]
        build_taps(taps_ref.at[part], weights, rows[HIGH_ROW : HIGH_ROW + 1], rows[LOW_ROW : LOW_ROW + 1])


def back_kernel(mine_ref, other_ref, data_ref, ctf_ref, cos_ref, sin_ref, taps_ref, out_ref, back):
    back[2 * RB :, :] = jnp.zeros((TIGHT - 2 * RB, ROWS), F32)
    for chunk in range(ROWS // 128):
        at = slice(128 * chunk, 128 * (chunk + 1))
        ctf = ctf_ref[:, at]
        cosine = cos_ref[:, at]
        sine = sin_ref[:, at]
        proj_re = mine_ref[:IM, at] + other_ref[:IM, at].astype(F32)
        proj_im = mine_ref[IM:, at] + other_ref[IM:, at].astype(F32)
        res_re = ctf * (cosine * proj_re - sine * proj_im) - data_ref[0, :, at].astype(F32)
        res_im = ctf * (sine * proj_re + cosine * proj_im) - data_ref[1, :, at].astype(F32)
        back[:RB, at] = (ctf * (cosine * res_re + sine * res_im))[:RB]
        back[RB : 2 * RB, at] = (ctf * (cosine * res_im - sine * res_re))[:RB]
    back_low = back[...].astype(BF16)
    group = lane_group((TIGHT, 128))
    for pair in range(4):
        grads = []
        for part in range(N_X):
            lines = taps_ref[part, 256 * pair : 256 * (pair + 1), :]
            grads.append(lax.dot_general(back_low, lines, (((1,), (1,)), ((), ())), preferred_element_type=F32))
        for side in range(2):
            tiles = [grad[:, 128 * side : 128 * (side + 1)] for grad in grads]
            for y, value in enumerate(regroup_all(tiles, group)):
                out_ref[4 * (2 * pair + side) + y] = value.astype(BF16)


def reduce_kernel(parts_ref, own_ref, grad_ref, cand_ref, total):
    total[...] = jnp.sum(parts_ref[...].astype(F32), axis=0)
    grad_ref[...] = jnp.zeros(grad_ref.shape, F32)
    grad_ref[:RB, :] = total[:RB, :]
    grad_ref[IM : IM + RB, :] = total[RB : 2 * RB, :]
    row = lax.broadcasted_iota(jnp.int32, cand_ref.shape, 0) % IM
    cand_ref[...] = jnp.where(row < RB, own_ref[...] - STEP * grad_ref[...], 0.0)


def split(value):
    high = value.astype(BF16).astype(F32)
    return high, value - high


def shell_kernel(grad_ref, cand_ref, other_ref, out_ref, block):
    mine = cand_ref[...]
    other = other_ref[...]
    for item, product in enumerate((mine * other, mine * mine, other * other)):
        shell = product[:IM] + product[IM:]
        shell = jnp.concatenate([shell, jnp.zeros((128 - IM, 128), F32)], axis=0)
        row = jnp.sum(shell.T, axis=0, keepdims=True)
        row = row + pltpu.roll(row, 64, 1)
        high, low = split(row)
        block[FOLD + 2 * item : FOLD + 2 * item + 1, :] = high
        block[FOLD + 2 * item + 1 : FOLD + 2 * item + 2, :] = low
    block[FOLD + 6 :, :] = jnp.zeros((32 - FOLD - 6, 128), F32)
    group = lane_group((FOLD, 128))
    tiles = [grad_ref[at : at + FOLD, :] for at in (0, FOLD, IM, IM + FOLD)]
    for slot, folded in enumerate(regroup_all(tiles, group)):
        block[:FOLD, :] = folded
        value = block[...].astype(BF16)
        out_ref[slot] = value
        out_ref[N_X + slot] = value


def share_kernel(parts_ref, out_ref, block, whole):
    first = (lax.axis_index("slab") >> 2) * N_X
    for part in range(N_X):
        block[part] = parts_ref[first + part].astype(F32)
    tiles = [block[part, :FOLD, :] for part in range(N_X)]
    group = lane_group((FOLD, 128))
    for at, value in zip((0, FOLD, IM, IM + FOLD), regroup_all(tiles, group), strict=True):
        whole[at : at + FOLD, :] = value
    for part in range(N_X):
        block[part] = parts_ref[part].astype(F32) + parts_ref[N_X + part].astype(F32)
    lane = lax.broadcasted_iota(jnp.int32, (1, 128), 1)
    for pair, at in enumerate(SUM_ROWS):
        for item in range(3):
            row = FOLD + 2 * item
            sums = [block[2 * pair + side, row : row + 1, :] + block[2 * pair + side, row + 1 : row + 2, :] for side in (0, 1)]
            high, low = split(jnp.where(lane < 64, sums[0], sums[1]))
            whole[at + 2 * item : at + 2 * item + 1, :] = high
            whole[at + 2 * item + 1 : at + 2 * item + 2, :] = low
    value = whole[...].astype(BF16)
    for dom in range(N_DOM):
        out_ref[dom] = value


def update_kernel(map_ref, parts_ref, out_hbm, out_ref, sums, scale, left):
    for pair, at in enumerate(SUM_TILES):
        total = parts_ref[0, at : at + 16].astype(F32)
        for dom in range(1, N_DOM):
            total += parts_ref[dom, at : at + 16].astype(F32)
        sums[16 * pair : 16 * (pair + 1), :] = total
    factors = []
    for pair in range(2):
        at = 16 * pair + SUM_ROWS[pair] - SUM_TILES[pair]
        num, den_mine, den_other = [sums[row : row + 1, :] + sums[row + 1 : row + 2, :] for row in (at, at + 2, at + 4)]
        fsc = num / (jnp.sqrt(den_mine * den_other) + 1e-06)
        factors.append(STEP * (1.0 + fsc) / 2.0)
    factors.append(jnp.zeros((128 - len(factors), 128), F32))
    scale[...] = jnp.concatenate(factors, axis=0).T
    group = lane_group((BLOCK, 128))

    copies = []
    for z in range(8):
        lanes = slice(128 * z, 128 * (z + 1))
        tiles = [parts_ref[4 * z + y].astype(F32) for y in range(4)]
        for part, value in enumerate(regroup_all(tiles, group)):
            side = 64 * (part % 2)
            weight = scale[side : side + IM, part // 2 : part // 2 + 1]
            for at, rows in ((RB * part, value[:IM]), (R + RB * part, value[IM:])):
                out_ref[at : at + RB, lanes] = map_ref[at : at + RB, lanes] - (weight * rows)[:RB]
        copies.append(pltpu.make_async_copy(out_ref.at[:, lanes], out_hbm.at[:, lanes], left.at[z]))
        copies[-1].start()
    for copy in copies:
        copy.wait()


def vmem():
    return pl.BlockSpec(memory_space=pltpu.VMEM)


def limit(mib):
    return pltpu.CompilerParams(vmem_limit_bytes=mib << 20)


def cost(flops, moved):
    return pl.CostEstimate(flops=flops, bytes_accessed=moved, transcendentals=0)


def exchange(value, axis, groups=None):
    return lax.all_to_all(value, axis, 0, 0, tiled=True, axis_index_groups=groups)


def line_terms(classes_local, shifts_local, defocus, radius):
    class_ids = jnp.arange(defocus.shape[0], dtype=jnp.int32)
    focus = jnp.sum(jnp.where(classes_local[:, None] == class_ids[None, :], defocus[None, :], 0.0), axis=1)
    ctf = -jnp.sin(CTF_GAIN * focus[None, :] * (radius[:, None] / R) ** 2 + PHASE_ZERO)
    ctf_rows = jnp.repeat(ctf, LPI, axis=1)
    theta = jnp.pi * jnp.arange(LPI, dtype=F32) / LPI
    theta_rows = jnp.tile(theta, classes_local.shape[0])
    shift_x = jnp.repeat(shifts_local[0].astype(F32), LPI)
    shift_y = jnp.repeat(shifts_local[1].astype(F32), LPI)
    along = shift_x * jnp.cos(theta_rows) + shift_y * jnp.sin(theta_rows)
    phase = 2.0 * jnp.pi * radius[:, None] * along[None, :] / (2.0 * R)
    return (ctf_rows, jnp.cos(phase), jnp.sin(phase))


def body(volume, images, tap_index, tap_weight, classes, shifts, defocus):
    map_t = volume[0].T
    data_t = images[0].T
    slab = lax.axis_index("slab")
    x = slab & 3
    runs = [[N_X * run + at for at in range(N_X)] for run in range(N_SLAB // N_X)]

    sent = jax.ShapeDtypeStruct((N_X, SENT, ROWS), BF16)
    parts = pl.pallas_call(
        project_kernel,
        out_shape=sent,
        in_specs=[vmem(), vmem(), pl.BlockSpec(memory_space=pl.ANY)],
        out_specs=pl.BlockSpec(memory_space=pl.ANY),
        scratch_shapes=[
            pltpu.VMEM((2 * R, LINES), F32),
            pltpu.VMEM((N_X * BLOCK, LINES), F32),
            pltpu.VMEM((LINES, ROWS), BF16),
            pltpu.VMEM((N_X, SENT, ROWS), BF16),
            pltpu.SemaphoreType.DMA((2 * N_X,)),
            pltpu.SemaphoreType.DMA((N_X,)),
        ],
        name="project",
    )(tap_index[0, 0], tap_weight[0, 0], map_t)
    parts = exchange(parts, "slab", runs)

    pad = ((0, IM - RB), (0, 0))
    radius = (RB * x + jnp.arange(RB)).astype(F32)
    ctf, cosine, sine = line_terms(classes[0], shifts[0], defocus, radius)
    ctf, cosine, sine = (jnp.pad(ctf, pad), jnp.pad(cosine, pad), jnp.pad(sine, pad))
    data = lax.dynamic_slice(data_t.reshape(2, R, ROWS), (0, RB * x, 0), (2, RB, ROWS))
    data = jnp.pad(data, ((0, 0),) + pad)
    parts, ctf, cosine, sine, data = lax.optimization_barrier((parts, ctf, cosine, sine, data))

    shard = jax.ShapeDtypeStruct((BLOCK, 128), F32)
    mine, low, own = pl.pallas_call(
        gather_kernel,
        out_shape=(
            jax.ShapeDtypeStruct((BLOCK, ROWS), F32),
            jax.ShapeDtypeStruct((BLOCK, ROWS), BF16),
            shard,
        ),
        in_specs=[vmem()],
        out_specs=(vmem(), vmem(), vmem()),
        compiler_params=limit(4),
        name="gather",
    )(parts)
    other = lax.ppermute(low, "slab", [(at, at ^ N_X) for at in range(N_SLAB)])
    taps = pl.pallas_call(
        taps_kernel,
        out_shape=jax.ShapeDtypeStruct((N_X, LINES, ROWS), BF16),
        in_specs=[vmem()],
        out_specs=vmem(),
        compiler_params=limit(16),
        cost_estimate=cost(1 << 24, 10 << 20),
        name="taps",
    )(parts)
    parts = pl.pallas_call(
        back_kernel,
        out_shape=jax.ShapeDtypeStruct((N_DOM, TIGHT, 128), BF16),
        in_specs=[vmem()] * 7,
        out_specs=vmem(),
        scratch_shapes=[pltpu.VMEM((TIGHT, ROWS), F32)],
        compiler_params=limit(16),
        name="back",
    )(mine, other, data, ctf, cosine, sine, taps)
    parts = exchange(parts, "dom")

    grad, cand = pl.pallas_call(
        reduce_kernel,
        out_shape=(shard, shard),
        in_specs=[vmem()] * 2,
        out_specs=(vmem(), vmem()),
        scratch_shapes=[pltpu.VMEM((TIGHT, 128), F32)],
        compiler_params=limit(4),
        name="reduce",
    )(parts, own)
    other = lax.ppermute(cand, "half", [(0, 1), (1, 0)])
    share = pl.pallas_call(
        shell_kernel,
        out_shape=jax.ShapeDtypeStruct((N_SLAB, 32, 128), BF16),
        in_specs=[vmem()] * 3,
        out_specs=vmem(),
        scratch_shapes=[pltpu.VMEM((32, 128), F32)],
        compiler_params=limit(2),
        name="shell",
    )(grad, cand, other)
    share = exchange(share, "slab")
    every = pl.pallas_call(
        share_kernel,
        out_shape=jax.ShapeDtypeStruct((N_DOM, BLOCK, 128), BF16),
        in_specs=[vmem()],
        out_specs=vmem(),
        scratch_shapes=[pltpu.VMEM((N_X, 32, 128), F32), pltpu.VMEM((BLOCK, 128), F32)],
        compiler_params=limit(4),
        name="share",
    )(share)
    every = exchange(every, "dom")
    result = pl.pallas_call(
        update_kernel,
        out_shape=jax.ShapeDtypeStruct((2 * R, LINES), F32),
        in_specs=[vmem(), vmem()],
        out_specs=pl.BlockSpec(memory_space=pl.ANY),
        scratch_shapes=[
            pltpu.VMEM((2 * R, LINES), F32),
            pltpu.VMEM((32, 128), F32),
            pltpu.VMEM((128, 128), F32),
            pltpu.SemaphoreType.DMA((8,)),
        ],
        compiler_params=limit(8),
        name="update",
    )(map_t, every)
    return result.T[None]


def solution(mesh):
    placed = (
        P("half", "slab", None),
        P("half", "dom", None),
        P("half", "slab", None, "dom"),
        P("half", "slab", None, "dom"),
        P("half", "dom"),
        P("half", None, "dom"),
        P(),
    )
    return jax.shard_map(
        body, mesh=mesh, in_specs=placed, out_specs=P("half", "slab", None), check_vma=False
    )
```

```python
import math

import jax
import jax.numpy as jnp
from jax import lax
from jax.experimental import pallas as pl
from jax.experimental.pallas import tpu as pltpu
from jax.sharding import PartitionSpec as P

LPI = 64
CTF_GAIN = 30.0
PHASE_ZERO = 0.1
STEP_SCALE = 0.5

R = 200
K = 8
N_SLAB = 8
N_X = 4
N_DOM = 32
LINES = 1024
ROWS = 1024
RB = R // N_X
SHARE = LINES // N_DOM
FOLD = RB // 2
STEP = STEP_SCALE / math.sqrt(ROWS * N_DOM * K / LINES)

F32 = jnp.float32
BF16 = jnp.bfloat16

IM = 56
BLOCK = 112
SENT = BLOCK + 8
TIGHT = 104
TAP_ROWS = (50, 51, 52, 53, 54, 55, 106, 107)
HIGH_ROW = 108
LOW_ROW = 109
SUM_ROWS = (50, 106)
SUM_TILES = (48, 96)
CHUNK = 16
PIECES = (0, 56, 104, 152, 200, 256, 304, 352, 400)


def lane_group(shape):
    return lax.broadcasted_iota(jnp.int32, shape, len(shape) - 1) // SHARE


def regroup(tiles, source, group):
    out = None
    for slot, tile in enumerate(tiles):
        moved = pltpu.roll(tile, (SHARE * (slot - source)) % 128, 1)
        out = moved if out is None else jnp.where(group == slot, moved, out)
    return out


def regroup_all(tiles, group):
    low = group < 2
    even = (group & 1) == 0
    half = [jnp.where(low, tiles[at], pltpu.roll(tiles[at + 2], 2 * SHARE, 1)) for at in range(2)]
    half += [jnp.where(low, pltpu.roll(tiles[at], 2 * SHARE, 1), tiles[at + 2]) for at in range(2)]
    out = []
    for at in (0, 2):
        out.append(jnp.where(even, half[at], pltpu.roll(half[at + 1], SHARE, 1)))
        out.append(jnp.where(even, pltpu.roll(half[at], 3 * SHARE, 1), half[at + 1]))
    return out


def build_taps(taps, weights, high, low):
    line = lax.broadcasted_iota(jnp.int32, (CHUNK, ROWS), 0).astype(F32)
    first = jnp.zeros((CHUNK, ROWS), F32)
    second = jnp.zeros((CHUNK, ROWS), F32)
    for tap in range(K):
        first += jnp.where(line == low + tap, weights[tap], 0.0)
        second += jnp.where(line + CHUNK == low + tap, weights[tap], 0.0)
    first = first.astype(BF16)
    second = second.astype(BF16)
    high = jnp.broadcast_to(high, (CHUNK, ROWS)).astype(BF16)
    none = jnp.zeros((CHUNK, ROWS), BF16)
    before = None
    for chunk in range(LINES // CHUNK):
        here = high == jnp.asarray(chunk, BF16)
        value = jnp.where(here, first, none)
        if before is not None:
            value = jnp.where(before, second, value)
        taps[CHUNK * chunk : CHUNK * (chunk + 1), :] = value
        before = here


def project_kernel(index_hbm, weight_hbm, map_hbm, out_hbm, index_ref, weight_ref, map_ref, block, taps, out_ref, arrived, left):
    first = pltpu.make_async_copy(index_hbm, index_ref, arrived.at[2 * N_X])
    second = pltpu.make_async_copy(weight_hbm, weight_ref, arrived.at[2 * N_X + 1])
    first.start()
    second.start()
    pieces = []
    for piece in range(2 * N_X):
        rows = slice(PIECES[piece], PIECES[piece + 1])
        pieces.append(pltpu.make_async_copy(map_hbm.at[rows], map_ref.at[rows], arrived.at[piece]))
    for part in range(N_X):
        pieces[part].start()
        pieces[N_X + part].start()
    first.wait()
    second.wait()
    index = index_ref[...]
    weight = weight_ref[...]
    base = jnp.min(index, axis=0, keepdims=True)
    place = lax.broadcasted_iota(jnp.int32, index.shape, 0)
    ordered = jnp.zeros(weight.shape, F32)
    for tap in range(K):
        ordered += jnp.where(place == index[tap : tap + 1] - base, weight[tap : tap + 1], 0.0)
    high = (base >> 4).astype(F32)
    low = (base & 15).astype(F32)
    weights = [ordered[tap : tap + 1] for tap in range(K)]
    build_taps(taps, weights, high, low)

    dom = lax.axis_index("dom")
    z = pl.multiple_of((dom >> 2) * 128, 128)
    y = dom & 3
    group = lane_group((8, 128))
    for part in range(N_X):
        at = BLOCK * part
        pieces[part].wait()
        pieces[N_X + part].wait()
        block[at + RB : at + IM, :] = jnp.zeros((IM - RB, LINES), F32)
        block[at + IM + RB : at + BLOCK, :] = jnp.zeros((IM - RB, LINES), F32)
        block[at : at + RB, :] = map_ref[RB * part : RB * (part + 1), :]
        block[at + IM : at + IM + RB, :] = map_ref[R + RB * part : R + RB * (part + 1), :]
        for lanes in range(LINES // 128):
            own = jnp.zeros((8, 128), F32)
            for slot in range(4):
                eight = 4 * lanes + slot
                if eight < BLOCK // 8:
                    tile = block[at + 8 * eight : at + 8 * eight + 8, pl.ds(z, 128)]
                    moved = pltpu.roll(tile, (SHARE * (slot - y)) & 127, 1)
                    own = jnp.where(group == slot, moved, own)
            out_ref[part, BLOCK:, 128 * lanes : 128 * (lanes + 1)] = own.astype(BF16)
    block[...] = jnp.dot(block[...].astype(BF16), taps[...], preferred_element_type=F32)
    for part in range(N_X):
        at = BLOCK * part
        for row, value in zip(TAP_ROWS + (HIGH_ROW, LOW_ROW), weights + [high, low], strict=True):
            block[at + row : at + row + 1, :] = value
        out_ref[part, :BLOCK, :] = block[at : at + BLOCK, :].astype(BF16)
        pltpu.make_async_copy(out_ref.at[part], out_hbm.at[part], left.at[part]).start()
    for part in range(N_X):
        pltpu.make_async_copy(out_ref.at[part], out_hbm.at[part], left.at[part]).wait()


def gather_kernel(parts_ref, mine_ref, low_ref, own_ref):
    total = parts_ref[0, :BLOCK].astype(F32)
    for part in range(1, N_X):
        total += parts_ref[part, :BLOCK].astype(F32)
    mine_ref[...] = total
    low_ref[...] = total.astype(BF16)
    group = lane_group((8, 128))
    for eight in range(BLOCK // 8):
        lanes = 128 * (eight // 4)
        tiles = [parts_ref[part, BLOCK:, lanes : lanes + 128].astype(F32) for part in range(N_X)]
        own_ref[8 * eight : 8 * eight + 8, :] = regroup(tiles, eight % 4, group)


def taps_kernel(parts_ref, taps_ref):
    @pl.loop(0, N_X)
    def _(part):
        rows = parts_ref[part].astype(F32)
        weights = [rows[row : row + 1] for row in TAP_ROWS]
        build_taps(taps_ref.at[part], weights, rows[HIGH_ROW : HIGH_ROW + 1], rows[LOW_ROW : LOW_ROW + 1])


def back_kernel(mine_ref, other_ref, data_ref, ctf_ref, cos_ref, sin_ref, taps_ref, out_ref, back, grad):
    back[2 * RB :, :] = jnp.zeros((TIGHT - 2 * RB, ROWS), F32)
    for chunk in range(ROWS // 128):
        at = slice(128 * chunk, 128 * (chunk + 1))
        ctf = ctf_ref[:, at]
        cosine = cos_ref[:, at]
        sine = sin_ref[:, at]
        proj_re = mine_ref[:IM, at] + other_ref[:IM, at].astype(F32)
        proj_im = mine_ref[IM:, at] + other_ref[IM:, at].astype(F32)
        res_re = ctf * (cosine * proj_re - sine * proj_im) - data_ref[0, :, at].astype(F32)
        res_im = ctf * (sine * proj_re + cosine * proj_im) - data_ref[1, :, at].astype(F32)
        back[:RB, at] = (ctf * (cosine * res_re + sine * res_im))[:RB]
        back[RB : 2 * RB, at] = (ctf * (cosine * res_im - sine * res_re))[:RB]
    back_low = back[...].astype(BF16)
    for part in range(N_X):
        grad[part] = lax.dot_general(taps_ref[part], back_low, (((1,), (1,)), ((), ())), preferred_element_type=F32)
    for dom in range(N_DOM):
        lines = [grad[part, SHARE * dom : SHARE * (dom + 1), :] for part in range(N_X)]
        out_ref[dom] = jnp.concatenate(lines, axis=0).T.astype(BF16)


def reduce_kernel(parts_ref, own_ref, grad_ref, cand_ref, total):
    total[...] = jnp.sum(parts_ref[...].astype(F32), axis=0)
    grad_ref[...] = jnp.zeros(grad_ref.shape, F32)
    grad_ref[:RB, :] = total[:RB, :]
    grad_ref[IM : IM + RB, :] = total[RB : 2 * RB, :]
    row = lax.broadcasted_iota(jnp.int32, cand_ref.shape, 0) % IM
    cand_ref[...] = jnp.where(row < RB, own_ref[...] - STEP * grad_ref[...], 0.0)


def split(value):
    high = value.astype(BF16).astype(F32)
    return high, value - high


def shell_kernel(grad_ref, cand_ref, other_ref, out_ref, block):
    mine = cand_ref[...]
    other = other_ref[...]
    for item, product in enumerate((mine * other, mine * mine, other * other)):
        shell = product[:IM] + product[IM:]
        shell = jnp.concatenate([shell, jnp.zeros((128 - IM, 128), F32)], axis=0)
        row = jnp.sum(shell.T, axis=0, keepdims=True)
        row = row + pltpu.roll(row, 64, 1)
        high, low = split(row)
        block[FOLD + 2 * item : FOLD + 2 * item + 1, :] = high
        block[FOLD + 2 * item + 1 : FOLD + 2 * item + 2, :] = low
    block[FOLD + 6 :, :] = jnp.zeros((32 - FOLD - 6, 128), F32)
    group = lane_group((FOLD, 128))
    tiles = [grad_ref[at : at + FOLD, :] for at in (0, FOLD, IM, IM + FOLD)]
    for slot, folded in enumerate(regroup_all(tiles, group)):
        block[:FOLD, :] = folded
        value = block[...].astype(BF16)
        out_ref[slot] = value
        out_ref[N_X + slot] = value


def share_kernel(parts_ref, out_ref, block, whole):
    first = (lax.axis_index("slab") >> 2) * N_X
    for part in range(N_X):
        block[part] = parts_ref[first + part].astype(F32)
    tiles = [block[part, :FOLD, :] for part in range(N_X)]
    group = lane_group((FOLD, 128))
    for at, value in zip((0, FOLD, IM, IM + FOLD), regroup_all(tiles, group), strict=True):
        whole[at : at + FOLD, :] = value
    for part in range(N_X):
        block[part] = parts_ref[part].astype(F32) + parts_ref[N_X + part].astype(F32)
    lane = lax.broadcasted_iota(jnp.int32, (1, 128), 1)
    for pair, at in enumerate(SUM_ROWS):
        for item in range(3):
            row = FOLD + 2 * item
            sums = [block[2 * pair + side, row : row + 1, :] + block[2 * pair + side, row + 1 : row + 2, :] for side in (0, 1)]
            high, low = split(jnp.where(lane < 64, sums[0], sums[1]))
            whole[at + 2 * item : at + 2 * item + 1, :] = high
            whole[at + 2 * item + 1 : at + 2 * item + 2, :] = low
    value = whole[...].astype(BF16)
    for dom in range(N_DOM):
        out_ref[dom] = value


def update_kernel(map_ref, parts_ref, out_hbm, out_ref, sums, scale, left):
    for pair, at in enumerate(SUM_TILES):
        total = parts_ref[0, at : at + 16].astype(F32)
        for dom in range(1, N_DOM):
            total += parts_ref[dom, at : at + 16].astype(F32)
        sums[16 * pair : 16 * (pair + 1), :] = total
    factors = []
    for pair in range(2):
        at = 16 * pair + SUM_ROWS[pair] - SUM_TILES[pair]
        num, den_mine, den_other = [sums[row : row + 1, :] + sums[row + 1 : row + 2, :] for row in (at, at + 2, at + 4)]
        fsc = num / (jnp.sqrt(den_mine * den_other) + 1e-06)
        factors.append(STEP * (1.0 + fsc) / 2.0)
    factors.append(jnp.zeros((128 - len(factors), 128), F32))
    scale[...] = jnp.concatenate(factors, axis=0).T
    group = lane_group((BLOCK, 128))

    copies = []
    for z in range(8):
        lanes = slice(128 * z, 128 * (z + 1))
        tiles = [parts_ref[4 * z + y].astype(F32) for y in range(4)]
        for part, value in enumerate(regroup_all(tiles, group)):
            side = 64 * (part % 2)
            weight = scale[side : side + IM, part // 2 : part // 2 + 1]
            for at, rows in ((RB * part, value[:IM]), (R + RB * part, value[IM:])):
                out_ref[at : at + RB, lanes] = map_ref[at : at + RB, lanes] - (weight * rows)[:RB]
        copies.append(pltpu.make_async_copy(out_ref.at[:, lanes], out_hbm.at[:, lanes], left.at[z]))
        copies[-1].start()
    for copy in copies:
        copy.wait()


def vmem():
    return pl.BlockSpec(memory_space=pltpu.VMEM)


def limit(mib):
    return pltpu.CompilerParams(vmem_limit_bytes=mib << 20)


def cost(flops, moved):
    return pl.CostEstimate(flops=flops, bytes_accessed=moved, transcendentals=0)


def exchange(value, axis, groups=None):
    return lax.all_to_all(value, axis, 0, 0, tiled=True, axis_index_groups=groups)


def line_terms(classes_local, shifts_local, defocus, radius):
    class_ids = jnp.arange(defocus.shape[0], dtype=jnp.int32)
    focus = jnp.sum(jnp.where(classes_local[:, None] == class_ids[None, :], defocus[None, :], 0.0), axis=1)
    ctf = -jnp.sin(CTF_GAIN * focus[None, :] * (radius[:, None] / R) ** 2 + PHASE_ZERO)
    ctf_rows = jnp.repeat(ctf, LPI, axis=1)
    theta = jnp.pi * jnp.arange(LPI, dtype=F32) / LPI
    theta_rows = jnp.tile(theta, classes_local.shape[0])
    shift_x = jnp.repeat(shifts_local[0].astype(F32), LPI)
    shift_y = jnp.repeat(shifts_local[1].astype(F32), LPI)
    along = shift_x * jnp.cos(theta_rows) + shift_y * jnp.sin(theta_rows)
    phase = 2.0 * jnp.pi * radius[:, None] * along[None, :] / (2.0 * R)
    return (ctf_rows, jnp.cos(phase), jnp.sin(phase))


def body(volume, images, tap_index, tap_weight, classes, shifts, defocus):
    map_t = volume[0].T
    data_t = images[0].T
    slab = lax.axis_index("slab")
    x = slab & 3
    runs = [[N_X * run + at for at in range(N_X)] for run in range(N_SLAB // N_X)]

    sent = jax.ShapeDtypeStruct((N_X, SENT, ROWS), BF16)
    parts = pl.pallas_call(
        project_kernel,
        out_shape=sent,
        in_specs=[pl.BlockSpec(memory_space=pl.ANY)] * 3,
        out_specs=pl.BlockSpec(memory_space=pl.ANY),
        scratch_shapes=[
            pltpu.VMEM((K, ROWS), jnp.int32),
            pltpu.VMEM((K, ROWS), F32),
            pltpu.VMEM((2 * R, LINES), F32),
            pltpu.VMEM((N_X * BLOCK, LINES), F32),
            pltpu.VMEM((LINES, ROWS), BF16),
            pltpu.VMEM((N_X, SENT, ROWS), BF16),
            pltpu.SemaphoreType.DMA((2 * N_X + 2,)),
            pltpu.SemaphoreType.DMA((N_X,)),
        ],
        name="project",
    )(tap_index[0, 0], tap_weight[0, 0], map_t)
    parts = exchange(parts, "slab", runs)

    pad = ((0, IM - RB), (0, 0))
    radius = (RB * x + jnp.arange(RB)).astype(F32)
    ctf, cosine, sine = line_terms(classes[0], shifts[0], defocus, radius)
    ctf, cosine, sine = (jnp.pad(ctf, pad), jnp.pad(cosine, pad), jnp.pad(sine, pad))
    data = lax.dynamic_slice(data_t.reshape(2, R, ROWS), (0, RB * x, 0), (2, RB, ROWS))
    data = jnp.pad(data, ((0, 0),) + pad)
    parts, ctf, cosine, sine, data = lax.optimization_barrier((parts, ctf, cosine, sine, data))

    shard = jax.ShapeDtypeStruct((BLOCK, 128), F32)
    mine, low, own = pl.pallas_call(
        gather_kernel,
        out_shape=(
            jax.ShapeDtypeStruct((BLOCK, ROWS), F32),
            jax.ShapeDtypeStruct((BLOCK, ROWS), BF16),
            shard,
        ),
        in_specs=[vmem()],
        out_specs=(vmem(), vmem(), vmem()),
        compiler_params=limit(4),
        name="gather",
    )(parts)
    other = lax.ppermute(low, "slab", [(at, at ^ N_X) for at in range(N_SLAB)])
    taps = pl.pallas_call(
        taps_kernel,
        out_shape=jax.ShapeDtypeStruct((N_X, LINES, ROWS), BF16),
        in_specs=[vmem()],
        out_specs=vmem(),
        compiler_params=limit(16),
        cost_estimate=cost(1 << 24, 10 << 20),
        name="taps",
    )(parts)
    parts = pl.pallas_call(
        back_kernel,
        out_shape=jax.ShapeDtypeStruct((N_DOM, TIGHT, 128), BF16),
        in_specs=[vmem()] * 7,
        out_specs=vmem(),
        scratch_shapes=[pltpu.VMEM((TIGHT, ROWS), F32), pltpu.VMEM((N_X, LINES, TIGHT), F32)],
        compiler_params=limit(16),
        name="back",
    )(mine, other, data, ctf, cosine, sine, taps)
    parts = exchange(parts, "dom")

    grad, cand = pl.pallas_call(
        reduce_kernel,
        out_shape=(shard, shard),
        in_specs=[vmem()] * 2,
        out_specs=(vmem(), vmem()),
        scratch_shapes=[pltpu.VMEM((TIGHT, 128), F32)],
        compiler_params=limit(4),
        name="reduce",
    )(parts, own)
    other = lax.ppermute(cand, "half", [(0, 1), (1, 0)])
    share = pl.pallas_call(
        shell_kernel,
        out_shape=jax.ShapeDtypeStruct((N_SLAB, 32, 128), BF16),
        in_specs=[vmem()] * 3,
        out_specs=vmem(),
        scratch_shapes=[pltpu.VMEM((32, 128), F32)],
        compiler_params=limit(2),
        name="shell",
    )(grad, cand, other)
    share = exchange(share, "slab")
    every = pl.pallas_call(
        share_kernel,
        out_shape=jax.ShapeDtypeStruct((N_DOM, BLOCK, 128), BF16),
        in_specs=[vmem()],
        out_specs=vmem(),
        scratch_shapes=[pltpu.VMEM((N_X, 32, 128), F32), pltpu.VMEM((BLOCK, 128), F32)],
        compiler_params=limit(4),
        name="share",
    )(share)
    every = exchange(every, "dom")
    result = pl.pallas_call(
        update_kernel,
        out_shape=jax.ShapeDtypeStruct((2 * R, LINES), F32),
        in_specs=[vmem(), vmem()],
        out_specs=pl.BlockSpec(memory_space=pl.ANY),
        scratch_shapes=[
            pltpu.VMEM((2 * R, LINES), F32),
            pltpu.VMEM((32, 128), F32),
            pltpu.VMEM((128, 128), F32),
            pltpu.SemaphoreType.DMA((8,)),
        ],
        compiler_params=limit(8),
        name="update",
    )(map_t, every)
    return result.T[None]


def solution(mesh):
    placed = (
        P("half", "slab", None),
        P("half", "dom", None),
        P("half", "slab", None, "dom"),
        P("half", "slab", None, "dom"),
        P("half", "dom"),
        P("half", None, "dom"),
        P(),
    )
    return jax.shard_map(
        body, mesh=mesh, in_specs=placed, out_specs=P("half", "slab", None), check_vma=False
    )
```

```python
import math

import jax
import jax.numpy as jnp
from jax import lax
from jax.experimental import pallas as pl
from jax.experimental.pallas import tpu as pltpu
from jax.sharding import PartitionSpec as P

LPI = 64
CTF_GAIN = 30.0
PHASE_ZERO = 0.1
STEP_SCALE = 0.5

R = 200
K = 8
N_SLAB = 8
N_X = 4
N_DOM = 32
LINES = 1024
ROWS = 1024
RB = R // N_X
SHARE = LINES // N_DOM
FOLD = RB // 2
STEP = STEP_SCALE / math.sqrt(ROWS * N_DOM * K / LINES)

F32 = jnp.float32
BF16 = jnp.bfloat16

IM = 56
BLOCK = 112
SENT = BLOCK + 8
TIGHT = 104
TAP_ROWS = (50, 51, 52, 53, 54, 55, 106, 107)
HIGH_ROW = 108
LOW_ROW = 109
SUM_ROWS = (50, 106)
SUM_TILES = (48, 96)
CHUNK = 16
PIECES = (0, 56, 104, 152, 200, 256, 304, 352, 400)


def lane_group(shape):
    return lax.broadcasted_iota(jnp.int32, shape, len(shape) - 1) // SHARE


def regroup(tiles, source, group):
    out = None
    for slot, tile in enumerate(tiles):
        moved = pltpu.roll(tile, (SHARE * (slot - source)) % 128, 1)
        out = moved if out is None else jnp.where(group == slot, moved, out)
    return out


def regroup_all(tiles, group):
    low = group < 2
    even = (group & 1) == 0
    half = [jnp.where(low, tiles[at], pltpu.roll(tiles[at + 2], 2 * SHARE, 1)) for at in range(2)]
    half += [jnp.where(low, pltpu.roll(tiles[at], 2 * SHARE, 1), tiles[at + 2]) for at in range(2)]
    out = []
    for at in (0, 2):
        out.append(jnp.where(even, half[at], pltpu.roll(half[at + 1], SHARE, 1)))
        out.append(jnp.where(even, pltpu.roll(half[at], 3 * SHARE, 1), half[at + 1]))
    return out


def build_taps(taps, weights, high, low):
    line = lax.broadcasted_iota(jnp.int32, (CHUNK, ROWS), 0).astype(F32)
    first = jnp.zeros((CHUNK, ROWS), F32)
    second = jnp.zeros((CHUNK, ROWS), F32)
    for tap in range(K):
        first += jnp.where(line == low + tap, weights[tap], 0.0)
        second += jnp.where(line + CHUNK == low + tap, weights[tap], 0.0)
    first = first.astype(BF16)
    second = second.astype(BF16)
    high = jnp.broadcast_to(high, (CHUNK, ROWS)).astype(BF16)
    none = jnp.zeros((CHUNK, ROWS), BF16)
    before = None
    for chunk in range(LINES // CHUNK):
        here = high == jnp.asarray(chunk, BF16)
        value = jnp.where(here, first, none)
        if before is not None:
            value = jnp.where(before, second, value)
        taps[CHUNK * chunk : CHUNK * (chunk + 1), :] = value
        before = here


def project_kernel(index_hbm, weight_hbm, map_hbm, out_hbm, index_ref, weight_ref, map_ref, block, taps, out_ref, arrived, left):
    first = pltpu.make_async_copy(index_hbm, index_ref, arrived.at[2 * N_X])
    second = pltpu.make_async_copy(weight_hbm, weight_ref, arrived.at[2 * N_X + 1])
    first.start()
    second.start()
    pieces = []
    for piece in range(2 * N_X):
        rows = slice(PIECES[piece], PIECES[piece + 1])
        pieces.append(pltpu.make_async_copy(map_hbm.at[rows], map_ref.at[rows], arrived.at[piece]))
    for part in range(N_X):
        pieces[part].start()
        pieces[N_X + part].start()
    first.wait()
    second.wait()
    index = index_ref[...]
    weight = weight_ref[...]
    base = jnp.min(index, axis=0, keepdims=True)
    place = lax.broadcasted_iota(jnp.int32, index.shape, 0)
    ordered = jnp.zeros(weight.shape, F32)
    for tap in range(K):
        ordered += jnp.where(place == index[tap : tap + 1] - base, weight[tap : tap + 1], 0.0)
    high = (base >> 4).astype(F32)
    low = (base & 15).astype(F32)
    weights = [ordered[tap : tap + 1] for tap in range(K)]
    build_taps(taps, weights, high, low)

    dom = lax.axis_index("dom")
    z = pl.multiple_of((dom >> 2) * 128, 128)
    y = dom & 3
    group = lane_group((8, 128))
    for part in range(N_X):
        at = BLOCK * part
        pieces[part].wait()
        pieces[N_X + part].wait()
        block[at + RB : at + IM, :] = jnp.zeros((IM - RB, LINES), F32)
        block[at + IM + RB : at + BLOCK, :] = jnp.zeros((IM - RB, LINES), F32)
        block[at : at + RB, :] = map_ref[RB * part : RB * (part + 1), :]
        block[at + IM : at + IM + RB, :] = map_ref[R + RB * part : R + RB * (part + 1), :]
        for lanes in range(LINES // 128):
            own = jnp.zeros((8, 128), F32)
            for slot in range(4):
                eight = 4 * lanes + slot
                if eight < BLOCK // 8:
                    tile = block[at + 8 * eight : at + 8 * eight + 8, pl.ds(z, 128)]
                    moved = pltpu.roll(tile, (SHARE * (slot - y)) & 127, 1)
                    own = jnp.where(group == slot, moved, own)
            out_ref[part, BLOCK:, 128 * lanes : 128 * (lanes + 1)] = own.astype(BF16)
    block[...] = jnp.dot(block[...].astype(BF16), taps[...], preferred_element_type=F32)
    for part in range(N_X):
        at = BLOCK * part
        for row, value in zip(TAP_ROWS + (HIGH_ROW, LOW_ROW), weights + [high, low], strict=True):
            block[at + row : at + row + 1, :] = value
        out_ref[part, :BLOCK, :] = block[at : at + BLOCK, :].astype(BF16)
        pltpu.make_async_copy(out_ref.at[part], out_hbm.at[part], left.at[part]).start()
    for part in range(N_X):
        pltpu.make_async_copy(out_ref.at[part], out_hbm.at[part], left.at[part]).wait()


def gather_kernel(parts_ref, mine_ref, low_ref, own_ref, tight):
    total = parts_ref[0, :BLOCK].astype(F32)
    for part in range(1, N_X):
        total += parts_ref[part, :BLOCK].astype(F32)
    mine_ref[...] = total
    tight[: TIGHT // 2, :] = total[: TIGHT // 2]
    tight[TIGHT // 2 :, :] = total[IM : IM + TIGHT // 2]
    low_ref[...] = tight[...].astype(BF16)
    group = lane_group((8, 128))
    for eight in range(BLOCK // 8):
        lanes = 128 * (eight // 4)
        tiles = [parts_ref[part, BLOCK:, lanes : lanes + 128].astype(F32) for part in range(N_X)]
        own_ref[8 * eight : 8 * eight + 8, :] = regroup(tiles, eight % 4, group)


def taps_kernel(parts_ref, taps_ref):
    @pl.loop(0, N_X)
    def _(part):
        rows = parts_ref[part].astype(F32)
        weights = [rows[row : row + 1] for row in TAP_ROWS]
        build_taps(taps_ref.at[part], weights, rows[HIGH_ROW : HIGH_ROW + 1], rows[LOW_ROW : LOW_ROW + 1])


def back_kernel(mine_ref, other_ref, data_ref, ctf_ref, cos_ref, sin_ref, taps_ref, out_ref, back, grad, theirs):
    back[2 * RB :, :] = jnp.zeros((TIGHT - 2 * RB, ROWS), F32)
    theirs[:, TIGHT:, :] = jnp.zeros((2, BLOCK - TIGHT, 128), F32)
    for chunk in range(ROWS // 128):
        at = slice(128 * chunk, 128 * (chunk + 1))
        ctf = ctf_ref[:, at]
        cosine = cos_ref[:, at]
        sine = sin_ref[:, at]
        theirs[chunk % 2, :TIGHT, :] = other_ref[:, at].astype(F32)
        proj_re = mine_ref[:IM, at] + theirs[chunk % 2, :IM, :]
        proj_im = mine_ref[IM:, at] + theirs[chunk % 2, TIGHT // 2 : TIGHT // 2 + IM, :]
        res_re = ctf * (cosine * proj_re - sine * proj_im) - data_ref[0, :, at].astype(F32)
        res_im = ctf * (sine * proj_re + cosine * proj_im) - data_ref[1, :, at].astype(F32)
        back[:RB, at] = (ctf * (cosine * res_re + sine * res_im))[:RB]
        back[RB : 2 * RB, at] = (ctf * (cosine * res_im - sine * res_re))[:RB]
    back_low = back[...].astype(BF16)
    for part in range(N_X):
        grad[part] = lax.dot_general(taps_ref[part], back_low, (((1,), (1,)), ((), ())), preferred_element_type=F32)
    for dom in range(N_DOM):
        lines = [grad[part, SHARE * dom : SHARE * (dom + 1), :] for part in range(N_X)]
        out_ref[dom] = jnp.concatenate(lines, axis=0).T.astype(BF16)


def reduce_kernel(parts_ref, own_ref, grad_ref, cand_ref, total):
    total[...] = jnp.sum(parts_ref[...].astype(F32), axis=0)
    grad_ref[...] = jnp.zeros(grad_ref.shape, F32)
    grad_ref[:RB, :] = total[:RB, :]
    grad_ref[IM : IM + RB, :] = total[RB : 2 * RB, :]
    row = lax.broadcasted_iota(jnp.int32, cand_ref.shape, 0) % IM
    cand_ref[...] = jnp.where(row < RB, own_ref[...] - STEP * grad_ref[...], 0.0)


def split(value):
    high = value.astype(BF16).astype(F32)
    return high, value - high


def shell_kernel(grad_ref, cand_ref, other_ref, out_ref, block):
    mine = cand_ref[...]
    other = other_ref[...]
    for item, product in enumerate((mine * other, mine * mine, other * other)):
        shell = product[:IM] + product[IM:]
        shell = jnp.concatenate([shell, jnp.zeros((128 - IM, 128), F32)], axis=0)
        row = jnp.sum(shell.T, axis=0, keepdims=True)
        row = row + pltpu.roll(row, 64, 1)
        high, low = split(row)
        block[FOLD + 2 * item : FOLD + 2 * item + 1, :] = high
        block[FOLD + 2 * item + 1 : FOLD + 2 * item + 2, :] = low
    block[FOLD + 6 :, :] = jnp.zeros((32 - FOLD - 6, 128), F32)
    group = lane_group((FOLD, 128))
    tiles = [grad_ref[at : at + FOLD, :] for at in (0, FOLD, IM, IM + FOLD)]
    for slot, folded in enumerate(regroup_all(tiles, group)):
        block[:FOLD, :] = folded
        value = block[...].astype(BF16)
        out_ref[slot] = value
        out_ref[N_X + slot] = value


def share_kernel(parts_ref, out_ref, block, whole):
    first = (lax.axis_index("slab") >> 2) * N_X
    for part in range(N_X):
        block[part] = parts_ref[first + part].astype(F32)
    tiles = [block[part, :FOLD, :] for part in range(N_X)]
    group = lane_group((FOLD, 128))
    for at, value in zip((0, FOLD, IM, IM + FOLD), regroup_all(tiles, group), strict=True):
        whole[at : at + FOLD, :] = value
    for part in range(N_X):
        block[part] = parts_ref[part].astype(F32) + parts_ref[N_X + part].astype(F32)
    lane = lax.broadcasted_iota(jnp.int32, (1, 128), 1)
    for pair, at in enumerate(SUM_ROWS):
        for item in range(3):
            row = FOLD + 2 * item
            sums = [block[2 * pair + side, row : row + 1, :] + block[2 * pair + side, row + 1 : row + 2, :] for side in (0, 1)]
            high, low = split(jnp.where(lane < 64, sums[0], sums[1]))
            whole[at + 2 * item : at + 2 * item + 1, :] = high
            whole[at + 2 * item + 1 : at + 2 * item + 2, :] = low
    value = whole[...].astype(BF16)
    for dom in range(N_DOM):
        out_ref[dom] = value


def update_kernel(map_ref, parts_ref, out_hbm, out_ref, sums, scale, left):
    for pair, at in enumerate(SUM_TILES):
        total = parts_ref[0, at : at + 16].astype(F32)
        for dom in range(1, N_DOM):
            total += parts_ref[dom, at : at + 16].astype(F32)
        sums[16 * pair : 16 * (pair + 1), :] = total
    factors = []
    for pair in range(2):
        at = 16 * pair + SUM_ROWS[pair] - SUM_TILES[pair]
        num, den_mine, den_other = [sums[row : row + 1, :] + sums[row + 1 : row + 2, :] for row in (at, at + 2, at + 4)]
        fsc = num / (jnp.sqrt(den_mine * den_other) + 1e-06)
        factors.append(STEP * (1.0 + fsc) / 2.0)
    factors.append(jnp.zeros((128 - len(factors), 128), F32))
    scale[...] = jnp.concatenate(factors, axis=0).T
    group = lane_group((BLOCK, 128))

    copies = []
    for z in range(8):
        lanes = slice(128 * z, 128 * (z + 1))
        tiles = [parts_ref[4 * z + y].astype(F32) for y in range(4)]
        for part, value in enumerate(regroup_all(tiles, group)):
            side = 64 * (part % 2)
            weight = scale[side : side + IM, part // 2 : part // 2 + 1]
            for at, rows in ((RB * part, value[:IM]), (R + RB * part, value[IM:])):
                out_ref[at : at + RB, lanes] = map_ref[at : at + RB, lanes] - (weight * rows)[:RB]
        copies.append(pltpu.make_async_copy(out_ref.at[:, lanes], out_hbm.at[:, lanes], left.at[z]))
        copies[-1].start()
    for copy in copies:
        copy.wait()


def vmem():
    return pl.BlockSpec(memory_space=pltpu.VMEM)


def limit(mib):
    return pltpu.CompilerParams(vmem_limit_bytes=mib << 20)


def cost(flops, moved):
    return pl.CostEstimate(flops=flops, bytes_accessed=moved, transcendentals=0)


def exchange(value, axis, groups=None):
    return lax.all_to_all(value, axis, 0, 0, tiled=True, axis_index_groups=groups)


def line_terms(classes_local, shifts_local, defocus, radius):
    class_ids = jnp.arange(defocus.shape[0], dtype=jnp.int32)
    focus = jnp.sum(jnp.where(classes_local[:, None] == class_ids[None, :], defocus[None, :], 0.0), axis=1)
    ctf = -jnp.sin(CTF_GAIN * focus[None, :] * (radius[:, None] / R) ** 2 + PHASE_ZERO)
    ctf_rows = jnp.repeat(ctf, LPI, axis=1)
    theta = jnp.pi * jnp.arange(LPI, dtype=F32) / LPI
    theta_rows = jnp.tile(theta, classes_local.shape[0])
    shift_x = jnp.repeat(shifts_local[0].astype(F32), LPI)
    shift_y = jnp.repeat(shifts_local[1].astype(F32), LPI)
    along = shift_x * jnp.cos(theta_rows) + shift_y * jnp.sin(theta_rows)
    phase = 2.0 * jnp.pi * radius[:, None] * along[None, :] / (2.0 * R)
    return (ctf_rows, jnp.cos(phase), jnp.sin(phase))


def body(volume, images, tap_index, tap_weight, classes, shifts, defocus):
    map_t = volume[0].T
    data_t = images[0].T
    slab = lax.axis_index("slab")
    x = slab & 3
    runs = [[N_X * run + at for at in range(N_X)] for run in range(N_SLAB // N_X)]

    sent = jax.ShapeDtypeStruct((N_X, SENT, ROWS), BF16)
    parts = pl.pallas_call(
        project_kernel,
        out_shape=sent,
        in_specs=[pl.BlockSpec(memory_space=pl.ANY)] * 3,
        out_specs=pl.BlockSpec(memory_space=pl.ANY),
        scratch_shapes=[
            pltpu.VMEM((K, ROWS), jnp.int32),
            pltpu.VMEM((K, ROWS), F32),
            pltpu.VMEM((2 * R, LINES), F32),
            pltpu.VMEM((N_X * BLOCK, LINES), F32),
            pltpu.VMEM((LINES, ROWS), BF16),
            pltpu.VMEM((N_X, SENT, ROWS), BF16),
            pltpu.SemaphoreType.DMA((2 * N_X + 2,)),
            pltpu.SemaphoreType.DMA((N_X,)),
        ],
        name="project",
    )(tap_index[0, 0], tap_weight[0, 0], map_t)
    parts = exchange(parts, "slab", runs)

    pad = ((0, IM - RB), (0, 0))
    radius = (RB * x + jnp.arange(RB)).astype(F32)
    ctf, cosine, sine = line_terms(classes[0], shifts[0], defocus, radius)
    ctf, cosine, sine = (jnp.pad(ctf, pad), jnp.pad(cosine, pad), jnp.pad(sine, pad))
    data = lax.dynamic_slice(data_t.reshape(2, R, ROWS), (0, RB * x, 0), (2, RB, ROWS))
    data = jnp.pad(data, ((0, 0),) + pad)
    parts, ctf, cosine, sine, data = lax.optimization_barrier((parts, ctf, cosine, sine, data))

    shard = jax.ShapeDtypeStruct((BLOCK, 128), F32)
    mine, low, own = pl.pallas_call(
        gather_kernel,
        out_shape=(
            jax.ShapeDtypeStruct((BLOCK, ROWS), F32),
            jax.ShapeDtypeStruct((TIGHT, ROWS), BF16),
            shard,
        ),
        in_specs=[vmem()],
        out_specs=(vmem(), vmem(), vmem()),
        scratch_shapes=[pltpu.VMEM((TIGHT, ROWS), F32)],
        compiler_params=limit(4),
        name="gather",
    )(parts)
    other = lax.ppermute(low, "slab", [(at, at ^ N_X) for at in range(N_SLAB)])
    taps = pl.pallas_call(
        taps_kernel,
        out_shape=jax.ShapeDtypeStruct((N_X, LINES, ROWS), BF16),
        in_specs=[vmem()],
        out_specs=vmem(),
        compiler_params=limit(16),
        cost_estimate=cost(1 << 24, 10 << 20),
        name="taps",
    )(parts)
    parts = pl.pallas_call(
        back_kernel,
        out_shape=jax.ShapeDtypeStruct((N_DOM, TIGHT, 128), BF16),
        in_specs=[vmem()] * 7,
        out_specs=vmem(),
        scratch_shapes=[pltpu.VMEM((TIGHT, ROWS), F32), pltpu.VMEM((N_X, LINES, TIGHT), F32), pltpu.VMEM((2, BLOCK, 128), F32)],
        compiler_params=limit(16),
        name="back",
    )(mine, other, data, ctf, cosine, sine, taps)
    parts = exchange(parts, "dom")

    grad, cand = pl.pallas_call(
        reduce_kernel,
        out_shape=(shard, shard),
        in_specs=[vmem()] * 2,
        out_specs=(vmem(), vmem()),
        scratch_shapes=[pltpu.VMEM((TIGHT, 128), F32)],
        compiler_params=limit(4),
        name="reduce",
    )(parts, own)
    other = lax.ppermute(cand, "half", [(0, 1), (1, 0)])
    share = pl.pallas_call(
        shell_kernel,
        out_shape=jax.ShapeDtypeStruct((N_SLAB, 32, 128), BF16),
        in_specs=[vmem()] * 3,
        out_specs=vmem(),
        scratch_shapes=[pltpu.VMEM((32, 128), F32)],
        compiler_params=limit(2),
        name="shell",
    )(grad, cand, other)
    share = exchange(share, "slab")
    every = pl.pallas_call(
        share_kernel,
        out_shape=jax.ShapeDtypeStruct((N_DOM, BLOCK, 128), BF16),
        in_specs=[vmem()],
        out_specs=vmem(),
        scratch_shapes=[pltpu.VMEM((N_X, 32, 128), F32), pltpu.VMEM((BLOCK, 128), F32)],
        compiler_params=limit(4),
        name="share",
    )(share)
    every = exchange(every, "dom")
    result = pl.pallas_call(
        update_kernel,
        out_shape=jax.ShapeDtypeStruct((2 * R, LINES), F32),
        in_specs=[vmem(), vmem()],
        out_specs=pl.BlockSpec(memory_space=pl.ANY),
        scratch_shapes=[
            pltpu.VMEM((2 * R, LINES), F32),
            pltpu.VMEM((32, 128), F32),
            pltpu.VMEM((128, 128), F32),
            pltpu.SemaphoreType.DMA((8,)),
        ],
        compiler_params=limit(8),
        name="update",
    )(map_t, every)
    return result.T[None]


def solution(mesh):
    placed = (
        P("half", "slab", None),
        P("half", "dom", None),
        P("half", "slab", None, "dom"),
        P("half", "slab", None, "dom"),
        P("half", "dom"),
        P("half", None, "dom"),
        P(),
    )
    return jax.shard_map(
        body, mesh=mesh, in_specs=placed, out_specs=P("half", "slab", None), check_vma=False
    )
```

```python
import math

import jax
import jax.numpy as jnp
from jax import lax
from jax.experimental import pallas as pl
from jax.experimental.pallas import tpu as pltpu
from jax.sharding import PartitionSpec as P

LPI = 64
CTF_GAIN = 30.0
PHASE_ZERO = 0.1
STEP_SCALE = 0.5

R = 200
K = 8
N_SLAB = 8
N_X = 4
N_DOM = 32
LINES = 1024
ROWS = 1024
RB = R // N_X
SHARE = LINES // N_DOM
FOLD = RB // 2
STEP = STEP_SCALE / math.sqrt(ROWS * N_DOM * K / LINES)

F32 = jnp.float32
BF16 = jnp.bfloat16

IM = 56
BLOCK = 112
SENT = BLOCK + 8
TIGHT = 104
TAP_ROWS = (50, 51, 52, 53, 54, 55, 106, 107)
HIGH_ROW = 108
LOW_ROW = 109
SUM_ROWS = (50, 106)
SUM_TILES = (48, 96)
CHUNK = 16
PIECES = (0, 56, 104, 152, 200, 256, 304, 352, 400)


def lane_group(shape):
    return lax.broadcasted_iota(jnp.int32, shape, len(shape) - 1) // SHARE


def regroup(tiles, source, group):
    out = None
    for slot, tile in enumerate(tiles):
        moved = pltpu.roll(tile, (SHARE * (slot - source)) % 128, 1)
        out = moved if out is None else jnp.where(group == slot, moved, out)
    return out


def regroup_all(tiles, group):
    low = group < 2
    even = (group & 1) == 0
    half = [jnp.where(low, tiles[at], pltpu.roll(tiles[at + 2], 2 * SHARE, 1)) for at in range(2)]
    half += [jnp.where(low, pltpu.roll(tiles[at], 2 * SHARE, 1), tiles[at + 2]) for at in range(2)]
    out = []
    for at in (0, 2):
        out.append(jnp.where(even, half[at], pltpu.roll(half[at + 1], SHARE, 1)))
        out.append(jnp.where(even, pltpu.roll(half[at], 3 * SHARE, 1), half[at + 1]))
    return out


def build_taps(taps, weights, high, low):
    line = lax.broadcasted_iota(jnp.int32, (CHUNK, ROWS), 0).astype(F32)
    first = jnp.zeros((CHUNK, ROWS), F32)
    second = jnp.zeros((CHUNK, ROWS), F32)
    for tap in range(K):
        first += jnp.where(line == low + tap, weights[tap], 0.0)
        second += jnp.where(line + CHUNK == low + tap, weights[tap], 0.0)
    first = first.astype(BF16)
    second = second.astype(BF16)
    high = jnp.broadcast_to(high, (CHUNK, ROWS)).astype(BF16)
    none = jnp.zeros((CHUNK, ROWS), BF16)
    before = None
    for chunk in range(LINES // CHUNK):
        here = high == jnp.asarray(chunk, BF16)
        value = jnp.where(here, first, none)
        if before is not None:
            value = jnp.where(before, second, value)
        taps[CHUNK * chunk : CHUNK * (chunk + 1), :] = value
        before = here


def project_kernel(index_hbm, weight_hbm, map_hbm, out_hbm, index_ref, weight_ref, map_ref, block, taps, out_ref, arrived, left):
    first = pltpu.make_async_copy(index_hbm, index_ref, arrived.at[2 * N_X])
    second = pltpu.make_async_copy(weight_hbm, weight_ref, arrived.at[2 * N_X + 1])
    first.start()
    second.start()
    pieces = []
    for piece in range(2 * N_X):
        rows = slice(PIECES[piece], PIECES[piece + 1])
        pieces.append(pltpu.make_async_copy(map_hbm.at[rows], map_ref.at[rows], arrived.at[piece]))
    for part in range(N_X):
        pieces[part].start()
        pieces[N_X + part].start()
    first.wait()
    second.wait()
    index = index_ref[...]
    weight = weight_ref[...]
    base = jnp.min(index, axis=0, keepdims=True)
    place = lax.broadcasted_iota(jnp.int32, index.shape, 0)
    ordered = jnp.zeros(weight.shape, F32)
    for tap in range(K):
        ordered += jnp.where(place == index[tap : tap + 1] - base, weight[tap : tap + 1], 0.0)
    high = (base >> 4).astype(F32)
    low = (base & 15).astype(F32)
    weights = [ordered[tap : tap + 1] for tap in range(K)]
    build_taps(taps, weights, high, low)

    dom = lax.axis_index("dom")
    z = pl.multiple_of((dom >> 2) * 128, 128)
    y = dom & 3
    group = lane_group((8, 128))
    for part in range(N_X):
        at = BLOCK * part
        pieces[part].wait()
        pieces[N_X + part].wait()
        block[at + RB : at + IM, :] = jnp.zeros((IM - RB, LINES), F32)
        block[at + IM + RB : at + BLOCK, :] = jnp.zeros((IM - RB, LINES), F32)
        block[at : at + RB, :] = map_ref[RB * part : RB * (part + 1), :]
        block[at + IM : at + IM + RB, :] = map_ref[R + RB * part : R + RB * (part + 1), :]
        for lanes in range(LINES // 128):
            own = jnp.zeros((8, 128), F32)
            for slot in range(4):
                eight = 4 * lanes + slot
                if eight < BLOCK // 8:
                    tile = block[at + 8 * eight : at + 8 * eight + 8, pl.ds(z, 128)]
                    moved = pltpu.roll(tile, (SHARE * (slot - y)) & 127, 1)
                    own = jnp.where(group == slot, moved, own)
            out_ref[part, BLOCK:, 128 * lanes : 128 * (lanes + 1)] = own.astype(BF16)
    block[...] = jnp.dot(block[...].astype(BF16), taps[...], preferred_element_type=F32)
    for part in range(N_X):
        at = BLOCK * part
        for row, value in zip(TAP_ROWS + (HIGH_ROW, LOW_ROW), weights + [high, low], strict=True):
            block[at + row : at + row + 1, :] = value
        out_ref[part, :BLOCK, :] = block[at : at + BLOCK, :].astype(BF16)
        pltpu.make_async_copy(out_ref.at[part], out_hbm.at[part], left.at[part]).start()
    for part in range(N_X):
        pltpu.make_async_copy(out_ref.at[part], out_hbm.at[part], left.at[part]).wait()


def gather_kernel(parts_ref, mine_ref, low_ref, own_ref, tight):
    total = parts_ref[0, :BLOCK].astype(F32)
    for part in range(1, N_X):
        total += parts_ref[part, :BLOCK].astype(F32)
    mine_ref[...] = total
    tight[: TIGHT // 2, :] = total[: TIGHT // 2]
    tight[TIGHT // 2 :, :] = total[IM : IM + TIGHT // 2]
    low_ref[...] = tight[...].astype(BF16)
    group = lane_group((8, 128))
    for eight in range(BLOCK // 8):
        lanes = 128 * (eight // 4)
        tiles = [parts_ref[part, BLOCK:, lanes : lanes + 128].astype(F32) for part in range(N_X)]
        own_ref[8 * eight : 8 * eight + 8, :] = regroup(tiles, eight % 4, group)


def taps_kernel(parts_ref, taps_ref):
    @pl.loop(0, N_X)
    def _(part):
        rows = parts_ref[part].astype(F32)
        weights = [rows[row : row + 1] for row in TAP_ROWS]
        build_taps(taps_ref.at[part], weights, rows[HIGH_ROW : HIGH_ROW + 1], rows[LOW_ROW : LOW_ROW + 1])


def back_kernel(mine_ref, other_ref, data_ref, ctf_ref, cos_ref, sin_ref, taps_ref, out_ref, back, grad, theirs):
    back[2 * RB :, :] = jnp.zeros((TIGHT - 2 * RB, ROWS), F32)
    theirs[:, TIGHT:, :] = jnp.zeros((2, BLOCK - TIGHT, 128), F32)
    for chunk in range(ROWS // 128):
        at = slice(128 * chunk, 128 * (chunk + 1))
        ctf = ctf_ref[:, at]
        cosine = cos_ref[:, at]
        sine = sin_ref[:, at]
        theirs[chunk % 2, :TIGHT, :] = other_ref[:, at].astype(F32)
        proj_re = mine_ref[:IM, at] + theirs[chunk % 2, :IM, :]
        proj_im = mine_ref[IM:, at] + theirs[chunk % 2, TIGHT // 2 : TIGHT // 2 + IM, :]
        res_re = ctf * (cosine * proj_re - sine * proj_im) - data_ref[0, :, at].astype(F32)
        res_im = ctf * (sine * proj_re + cosine * proj_im) - data_ref[1, :, at].astype(F32)
        back[:RB, at] = (ctf * (cosine * res_re + sine * res_im))[:RB]
        back[RB : 2 * RB, at] = (ctf * (cosine * res_im - sine * res_re))[:RB]
    back_low = back[...].astype(BF16)
    for part in range(N_X):
        grad[part] = lax.dot_general(taps_ref[part], back_low, (((1,), (1,)), ((), ())), preferred_element_type=F32)
    for dom in range(N_DOM):
        lines = [grad[part, SHARE * dom : SHARE * (dom + 1), :] for part in range(N_X)]
        out_ref[dom] = jnp.concatenate(lines, axis=0).T.astype(BF16)


def reduce_kernel(parts_ref, own_ref, grad_ref, cand_ref, low_ref, total):
    total[...] = jnp.sum(parts_ref[...].astype(F32), axis=0)
    grad_ref[...] = jnp.zeros(grad_ref.shape, F32)
    grad_ref[:RB, :] = total[:RB, :]
    grad_ref[IM : IM + RB, :] = total[RB : 2 * RB, :]
    row = lax.broadcasted_iota(jnp.int32, cand_ref.shape, 0) % IM
    cand = jnp.where(row < RB, own_ref[...] - STEP * grad_ref[...], 0.0)
    cand_ref[...] = cand
    low_ref[...] = cand.astype(BF16)


def split(value):
    high = value.astype(BF16).astype(F32)
    return high, value - high


def shell_kernel(grad_ref, cand_ref, other_ref, out_ref, block):
    mine = cand_ref[...]
    other = other_ref[...].astype(F32)
    for item, product in enumerate((mine * other, mine * mine, other * other)):
        shell = product[:IM] + product[IM:]
        shell = jnp.concatenate([shell, jnp.zeros((128 - IM, 128), F32)], axis=0)
        row = jnp.sum(shell.T, axis=0, keepdims=True)
        row = row + pltpu.roll(row, 64, 1)
        high, low = split(row)
        block[FOLD + 2 * item : FOLD + 2 * item + 1, :] = high
        block[FOLD + 2 * item + 1 : FOLD + 2 * item + 2, :] = low
    block[FOLD + 6 :, :] = jnp.zeros((32 - FOLD - 6, 128), F32)
    group = lane_group((FOLD, 128))
    tiles = [grad_ref[at : at + FOLD, :] for at in (0, FOLD, IM, IM + FOLD)]
    for slot, folded in enumerate(regroup_all(tiles, group)):
        block[:FOLD, :] = folded
        value = block[...].astype(BF16)
        out_ref[slot] = value
        out_ref[N_X + slot] = value


def share_kernel(parts_ref, out_ref, block, whole):
    first = (lax.axis_index("slab") >> 2) * N_X
    for part in range(N_X):
        block[part] = parts_ref[first + part].astype(F32)
    tiles = [block[part, :FOLD, :] for part in range(N_X)]
    group = lane_group((FOLD, 128))
    for at, value in zip((0, FOLD, IM, IM + FOLD), regroup_all(tiles, group), strict=True):
        whole[at : at + FOLD, :] = value
    for part in range(N_X):
        block[part] = parts_ref[part].astype(F32) + parts_ref[N_X + part].astype(F32)
    lane = lax.broadcasted_iota(jnp.int32, (1, 128), 1)
    for pair, at in enumerate(SUM_ROWS):
        for item in range(3):
            row = FOLD + 2 * item
            sums = [block[2 * pair + side, row : row + 1, :] + block[2 * pair + side, row + 1 : row + 2, :] for side in (0, 1)]
            high, low = split(jnp.where(lane < 64, sums[0], sums[1]))
            whole[at + 2 * item : at + 2 * item + 1, :] = high
            whole[at + 2 * item + 1 : at + 2 * item + 2, :] = low
    value = whole[...].astype(BF16)
    for dom in range(N_DOM):
        out_ref[dom] = value


def update_kernel(map_ref, parts_ref, out_hbm, out_ref, sums, scale, left):
    for pair, at in enumerate(SUM_TILES):
        total = parts_ref[0, at : at + 16].astype(F32)
        for dom in range(1, N_DOM):
            total += parts_ref[dom, at : at + 16].astype(F32)
        sums[16 * pair : 16 * (pair + 1), :] = total
    factors = []
    for pair in range(2):
        at = 16 * pair + SUM_ROWS[pair] - SUM_TILES[pair]
        num, den_mine, den_other = [sums[row : row + 1, :] + sums[row + 1 : row + 2, :] for row in (at, at + 2, at + 4)]
        fsc = num / (jnp.sqrt(den_mine * den_other) + 1e-06)
        factors.append(STEP * (1.0 + fsc) / 2.0)
    factors.append(jnp.zeros((128 - len(factors), 128), F32))
    scale[...] = jnp.concatenate(factors, axis=0).T
    group = lane_group((BLOCK, 128))

    copies = []
    for z in range(8):
        lanes = slice(128 * z, 128 * (z + 1))
        tiles = [parts_ref[4 * z + y].astype(F32) for y in range(4)]
        for part, value in enumerate(regroup_all(tiles, group)):
            side = 64 * (part % 2)
            weight = scale[side : side + IM, part // 2 : part // 2 + 1]
            for at, rows in ((RB * part, value[:IM]), (R + RB * part, value[IM:])):
                out_ref[at : at + RB, lanes] = map_ref[at : at + RB, lanes] - (weight * rows)[:RB]
        copies.append(pltpu.make_async_copy(out_ref.at[:, lanes], out_hbm.at[:, lanes], left.at[z]))
        copies[-1].start()
    for copy in copies:
        copy.wait()


def vmem():
    return pl.BlockSpec(memory_space=pltpu.VMEM)


def limit(mib):
    return pltpu.CompilerParams(vmem_limit_bytes=mib << 20)


def cost(flops, moved):
    return pl.CostEstimate(flops=flops, bytes_accessed=moved, transcendentals=0)


def exchange(value, axis, groups=None):
    return lax.all_to_all(value, axis, 0, 0, tiled=True, axis_index_groups=groups)


def line_terms(classes_local, shifts_local, defocus, radius):
    class_ids = jnp.arange(defocus.shape[0], dtype=jnp.int32)
    focus = jnp.sum(jnp.where(classes_local[:, None] == class_ids[None, :], defocus[None, :], 0.0), axis=1)
    ctf = -jnp.sin(CTF_GAIN * focus[None, :] * (radius[:, None] / R) ** 2 + PHASE_ZERO)
    ctf_rows = jnp.repeat(ctf, LPI, axis=1)
    theta = jnp.pi * jnp.arange(LPI, dtype=F32) / LPI
    theta_rows = jnp.tile(theta, classes_local.shape[0])
    shift_x = jnp.repeat(shifts_local[0].astype(F32), LPI)
    shift_y = jnp.repeat(shifts_local[1].astype(F32), LPI)
    along = shift_x * jnp.cos(theta_rows) + shift_y * jnp.sin(theta_rows)
    phase = 2.0 * jnp.pi * radius[:, None] * along[None, :] / (2.0 * R)
    return (ctf_rows, jnp.cos(phase), jnp.sin(phase))


def body(volume, images, tap_index, tap_weight, classes, shifts, defocus):
    map_t = volume[0].T
    data_t = images[0].T
    slab = lax.axis_index("slab")
    x = slab & 3
    runs = [[N_X * run + at for at in range(N_X)] for run in range(N_SLAB // N_X)]

    sent = jax.ShapeDtypeStruct((N_X, SENT, ROWS), BF16)
    parts = pl.pallas_call(
        project_kernel,
        out_shape=sent,
        in_specs=[pl.BlockSpec(memory_space=pl.ANY)] * 3,
        out_specs=pl.BlockSpec(memory_space=pl.ANY),
        scratch_shapes=[
            pltpu.VMEM((K, ROWS), jnp.int32),
            pltpu.VMEM((K, ROWS), F32),
            pltpu.VMEM((2 * R, LINES), F32),
            pltpu.VMEM((N_X * BLOCK, LINES), F32),
            pltpu.VMEM((LINES, ROWS), BF16),
            pltpu.VMEM((N_X, SENT, ROWS), BF16),
            pltpu.SemaphoreType.DMA((2 * N_X + 2,)),
            pltpu.SemaphoreType.DMA((N_X,)),
        ],
        name="project",
    )(tap_index[0, 0], tap_weight[0, 0], map_t)
    parts = exchange(parts, "slab", runs)

    pad = ((0, IM - RB), (0, 0))
    radius = (RB * x + jnp.arange(RB)).astype(F32)
    ctf, cosine, sine = line_terms(classes[0], shifts[0], defocus, radius)
    ctf, cosine, sine = (jnp.pad(ctf, pad), jnp.pad(cosine, pad), jnp.pad(sine, pad))
    data = lax.dynamic_slice(data_t.reshape(2, R, ROWS), (0, RB * x, 0), (2, RB, ROWS))
    data = jnp.pad(data, ((0, 0),) + pad)
    parts, ctf, cosine, sine, data = lax.optimization_barrier((parts, ctf, cosine, sine, data))

    shard = jax.ShapeDtypeStruct((BLOCK, 128), F32)
    mine, low, own = pl.pallas_call(
        gather_kernel,
        out_shape=(
            jax.ShapeDtypeStruct((BLOCK, ROWS), F32),
            jax.ShapeDtypeStruct((TIGHT, ROWS), BF16),
            shard,
        ),
        in_specs=[vmem()],
        out_specs=(vmem(), vmem(), vmem()),
        scratch_shapes=[pltpu.VMEM((TIGHT, ROWS), F32)],
        compiler_params=limit(4),
        name="gather",
    )(parts)
    other = lax.ppermute(low, "slab", [(at, at ^ N_X) for at in range(N_SLAB)])
    taps = pl.pallas_call(
        taps_kernel,
        out_shape=jax.ShapeDtypeStruct((N_X, LINES, ROWS), BF16),
        in_specs=[vmem()],
        out_specs=vmem(),
        compiler_params=limit(16),
        cost_estimate=cost(1 << 24, 10 << 20),
        name="taps",
    )(parts)
    parts = pl.pallas_call(
        back_kernel,
        out_shape=jax.ShapeDtypeStruct((N_DOM, TIGHT, 128), BF16),
        in_specs=[vmem()] * 7,
        out_specs=vmem(),
        scratch_shapes=[pltpu.VMEM((TIGHT, ROWS), F32), pltpu.VMEM((N_X, LINES, TIGHT), F32), pltpu.VMEM((2, BLOCK, 128), F32)],
        compiler_params=limit(16),
        name="back",
    )(mine, other, data, ctf, cosine, sine, taps)
    parts = exchange(parts, "dom")

    grad, cand, low = pl.pallas_call(
        reduce_kernel,
        out_shape=(shard, shard, jax.ShapeDtypeStruct((BLOCK, 128), BF16)),
        in_specs=[vmem()] * 2,
        out_specs=(vmem(), vmem(), vmem()),
        scratch_shapes=[pltpu.VMEM((TIGHT, 128), F32)],
        compiler_params=limit(4),
        name="reduce",
    )(parts, own)
    other = lax.ppermute(low, "half", [(0, 1), (1, 0)])
    share = pl.pallas_call(
        shell_kernel,
        out_shape=jax.ShapeDtypeStruct((N_SLAB, 32, 128), BF16),
        in_specs=[vmem()] * 3,
        out_specs=vmem(),
        scratch_shapes=[pltpu.VMEM((32, 128), F32)],
        compiler_params=limit(2),
        name="shell",
    )(grad, cand, other)
    share = exchange(share, "slab")
    every = pl.pallas_call(
        share_kernel,
        out_shape=jax.ShapeDtypeStruct((N_DOM, BLOCK, 128), BF16),
        in_specs=[vmem()],
        out_specs=vmem(),
        scratch_shapes=[pltpu.VMEM((N_X, 32, 128), F32), pltpu.VMEM((BLOCK, 128), F32)],
        compiler_params=limit(4),
        name="share",
    )(share)
    every = exchange(every, "dom")
    result = pl.pallas_call(
        update_kernel,
        out_shape=jax.ShapeDtypeStruct((2 * R, LINES), F32),
        in_specs=[vmem(), vmem()],
        out_specs=pl.BlockSpec(memory_space=pl.ANY),
        scratch_shapes=[
            pltpu.VMEM((2 * R, LINES), F32),
            pltpu.VMEM((32, 128), F32),
            pltpu.VMEM((128, 128), F32),
            pltpu.SemaphoreType.DMA((8,)),
        ],
        compiler_params=limit(8),
        name="update",
    )(map_t, every)
    return result.T[None]


def solution(mesh):
    placed = (
        P("half", "slab", None),
        P("half", "dom", None),
        P("half", "slab", None, "dom"),
        P("half", "slab", None, "dom"),
        P("half", "dom"),
        P("half", None, "dom"),
        P(),
    )
    return jax.shard_map(
        body, mesh=mesh, in_specs=placed, out_specs=P("half", "slab", None), check_vma=False
    )
```
